32 devices in a mesh: dp: 16 (over z, y, core), ctx: 2 (over x).
Axes of the slice: x: 2, y: 2, z: 4, core: 2. Of those that a mesh axis runs over, the one named last changes fastest.
Arguments:
- conv_input: bfloat16 [16, 256, 4096], P('dp', 'ctx'), may hold values from -6 to 6
- gate_value: bfloat16 [16, 256, 4096], P('dp', 'ctx'), may hold values from -6 to 6
- out_grad: bfloat16 [16, 256, 4096], P('dp', 'ctx'), may hold values from -6 to 6
- filter_taps: bfloat16 [128, 4096], P('dp'), may hold values from -0.5 to 0.5
Outputs:
- input_grad: bfloat16 [16, 256, 4096], P('dp', 'ctx')
- filter_grad: float32 [128, 4096], P('dp')
The draws below stay inside these ranges and needn't reach their ends.
All inputs are finite; a program needn't handle non-finite values.
Results may differ from the reference program's by a relative error of at most 0.0051.
Values may be sent and summed in bfloat16 or wider, within the bound.
A program may use at most 64 MiB of HBM per device.

```python
import math
import jax
import jax.numpy as jnp
from jax import lax

CHANNELS = 4096
TAPS = 128
SEQ = 256
SEQS = 16
TOKENS = 4096


def level_of(key, dims, pieces, low, high):
    level, own = 1.0, jax.random.fold_in(key, 6)
    for position, parts in pieces:
        steps = jnp.exp(jax.random.uniform(jax.random.fold_in(own, position), (parts,), jnp.float32, low / len(pieces), high / len(pieces)))
        level = level * jnp.repeat(steps, dims[position] // parts).reshape([-1 if axis == position else 1 for axis in range(len(dims))])
    return level


def gaussian(stream_key, dims, width, limit, cuts=(), held_as=jnp.bfloat16):
    array = jax.random.normal(stream_key, dims, jnp.float32) * width
    if len(cuts) > 0:
        array = level_of(stream_key, dims, cuts, -0.22, 0.18) * array
    return jnp.clip(array, min=-limit, max=limit).astype(held_as)


def setup_inputs(seed: int = 0) -> dict:
    arg_keys = jax.random.split(jax.random.key(seed), 5)
    conv_input = gaussian(arg_keys[0], (SEQS, SEQ, CHANNELS), 1.0, 6.0, ((0, 16), (1, 2)))
    gate_value = gaussian(arg_keys[1], (SEQS, SEQ, CHANNELS), 1.0, 6.0, ((0, 16), (1, 2)))
    out_grad = gaussian(arg_keys[2], (SEQS, SEQ, CHANNELS), 1.0, 6.0, ((0, 16), (1, 2)))
    filter_taps = gaussian(arg_keys[3], (TAPS, CHANNELS), TAPS ** -0.5, 0.5, ((0, 16),))
    return dict(conv_input=conv_input, gate_value=gate_value, out_grad=out_grad, filter_taps=filter_taps)


def reference(conv_input, gate_value, out_grad, filter_taps):
    mixed_grad = (out_grad.astype(jnp.float32) * gate_value.astype(jnp.float32)).astype(jnp.bfloat16)
    taps_wide = filter_taps.astype(jnp.float32)

    def one_sequence(pair):
        inputs, mixed = pair
        padded = jnp.concatenate([mixed, jnp.zeros((TAPS - 1, mixed.shape[1]), mixed.dtype)], 0)
        inputs_wide = inputs.astype(jnp.float32)

        def step(index, carry):
            total, grads = carry
            offset = jnp.asarray(index).astype(jnp.int32)
            window = lax.dynamic_slice_in_dim(padded, offset, SEQ, 0).astype(jnp.float32)
            tap_row = lax.dynamic_slice_in_dim(taps_wide, offset, 1, 0)
            total = total + tap_row * window
            grad_row = lax.optimization_barrier(jnp.sum(inputs_wide * window, 0, keepdims=True))
            grads = lax.dynamic_update_slice_in_dim(grads, grad_row, offset, 0)
            return (total, grads)
        start = (jnp.zeros((SEQ, mixed.shape[1]), jnp.float32), jnp.zeros((TAPS, mixed.shape[1]), jnp.float32))
        total, grads = lax.fori_loop(0, TAPS, step, start)
        return (total.astype(jnp.bfloat16), grads)
    input_grad, per_sequence = lax.map(one_sequence, (conv_input, mixed_grad))
    filter_grad = lax.optimization_barrier(jnp.sum(per_sequence, 0)) / math.sqrt(TOKENS)
    return (input_grad, filter_grad)
```

```python
import functools
import math

import jax
import jax.numpy as jnp
import numpy as np
from jax import lax
from jax.experimental import pallas as pl
from jax.experimental.pallas import tpu as pltpu
from jax.sharding import PartitionSpec as P


def split(values):
    high = values.astype(jnp.bfloat16)
    return high, (values - high.astype(np.float32)).astype(jnp.bfloat16)


def transforms(length):
    half = length // 2
    angle = np.pi * np.outer(2 * np.arange(half) + 1, np.arange(length)) / length
    forward = np.concatenate([np.cos(angle), -np.sin(angle)], 0)
    inverse = np.concatenate([np.cos(angle), -np.sin(angle)], 0).T / half
    return split(forward.astype(np.float32)), split(inverse.astype(np.float32))


def dot(a, b):
    return lax.dot_general(a, b, (((1,), (0,)), ((), ())), preferred_element_type=jnp.float32)


def general(conv_input, gate_value, out_grad, filter_taps):
    inputs = conv_input[0]
    rows = inputs.shape[0]
    taps = filter_taps.shape[0] * lax.axis_size("dp")
    (fh, fl), (bh, bl) = transforms(rows + taps)
    half = (rows + taps) // 2
    mixed = (out_grad[0].astype(jnp.float32) * gate_value[0].astype(jnp.float32)).astype(
        jnp.bfloat16
    )
    devices = lax.axis_size("ctx")
    rim = lax.ppermute(mixed[:taps], "ctx", [(i + 1, i) for i in range(devices - 1)])
    full_taps = lax.all_gather(filter_taps, "dp", axis=0, tiled=True)

    def spectrum(x, first=0):
        n = x.shape[0]
        s = dot(fh[:, first : first + n], x) + dot(fl[:, first : first + n], x)
        return s[:half], s[half:]

    def back(re, im, n):
        s = jnp.concatenate([re, im], 0)
        high = s.astype(jnp.bfloat16)
        low = (s - high.astype(jnp.float32)).astype(jnp.bfloat16)
        return dot(bh[:n], high) + dot(bl[:n], high) + dot(bh[:n], low)

    xr, xi = spectrum(inputs)
    gr0, gi0 = spectrum(mixed)
    gr1, gi1 = spectrum(rim, rows)
    gr, gi = gr0 + gr1, gi0 + gi1
    partial = back(xr * gr + xi * gi, xr * gi - xi * gr, taps)
    hr, hi = spectrum(full_taps)
    grad = back(hr * gr + hi * gi, hr * gi - hi * gr, rows)
    shard_grad = lax.psum(lax.psum_scatter(partial, "dp", scatter_dimension=0, tiled=True), "ctx")
    tokens_all = rows * devices * lax.axis_size("dp")
    return (grad.astype(jnp.bfloat16)[None], shard_grad * (1.0 / math.sqrt(tokens_all)))


CHUNKS = 8
MESH = pl.DeviceIdType.MESH


def kernel(
    pairs, ranks, scale,
    in_hbm, gate_hbm, cot_hbm, taps_hbm, f_hbm, b_hbm,
    obuf, fbuf,
    x_gate, x_cot, x_ext, g_ext, taps_all, f_all, b_all, p32, own32, csrc, cbuf, half32, ysrc, ybuf,
    zsrc, zbuf, xbuf,
    ld_in, ld_gate, ld_cot, ld_taps, ld_f,
    rim_s, rim_r, in_s, in_r, tz_s, ty_s, tc_s, tap_r,
    c_s, c_r, y_s, y_r, z_s, z_r, x_s, x_r,
):
    dp, ctx = lax.axis_index("dp"), lax.axis_index("ctx")
    core, mine = lax.rem(dp, 2), dp // 2
    partner = dp + 1 - 2 * core
    side, place, places = lax.rem(mine, 2), mine // 2, pairs // 2
    across = 2 * (mine + 1 - 2 * side) + core
    rows, channels = x_gate.shape
    wide = channels // CHUNKS
    middle = CHUNKS // 2
    last, first = ctx == ranks - 1, ctx == 0
    left, right = lax.max(ctx - 1, 0), lax.min(ctx + 1, ranks - 1)
    upper, lower = pl.ds(0, rows), pl.ds(rows, rows)

    def cols(c):
        return pl.ds(pl.multiple_of(c * wide, wide), wide)

    def load(src, dst, sem, c):
        return pltpu.make_async_copy(src.at[:, cols(c)], dst.at[:, cols(c)], sem.at[c])

    def load_in(c):
        return pltpu.make_async_copy(in_hbm.at[:, cols(c)], x_ext.at[lower, cols(c)], ld_in.at[c])

    def each(n, body, start=0):
        lax.fori_loop(start, n, lambda i, z: (body(i), z)[1], 0)

    own_taps = pltpu.make_async_copy(taps_hbm, taps_all.at[dp], ld_taps)
    load_f = pltpu.make_async_copy(f_hbm, f_all, ld_f.at[0])
    load_b = pltpu.make_async_copy(b_hbm, b_all, ld_f.at[1])

    def loads(c):
        load(cot_hbm, x_cot, ld_cot, c).start()
        load(gate_hbm, x_gate, ld_gate, c).start()

    each(CHUNKS, loads)
    own_taps.start()
    load_f.start()
    load_b.start()
    each(CHUNKS, lambda c: load_in(c).start())

    def z_peer(k):
        return lax.rem(place + k, places)

    def z_device(k):
        return 4 * z_peer(k) + 2 * side + core

    def rank(k):
        return lax.rem(ctx + k, ranks)

    barrier = pltpu.get_barrier_semaphore()
    pl.semaphore_signal(barrier, inc=1, device_id=(partner, ctx), device_id_type=MESH)
    pl.semaphore_signal(barrier, inc=1, device_id=(across, ctx), device_id_type=MESH)
    for k in range(1, places):
        pl.semaphore_signal(barrier, inc=1, device_id=(z_device(k), ctx), device_id_type=MESH)
    for k in range(1, ranks):
        pl.semaphore_signal(barrier, inc=1, device_id=(dp, rank(k)), device_id_type=MESH)
    def remote(src, dst, send, recv, to):
        return pltpu.make_async_remote_copy(
            src_ref=src, dst_ref=dst, send_sem=send, recv_sem=recv, device_id=to, device_id_type=MESH
        )

    def rim(c):
        return remote(g_ext.at[upper, cols(c)], g_ext.at[lower, cols(c)], rim_s.at[c], rim_r.at[c], (dp, left))

    def lend(c):
        return remote(in_hbm.at[:, cols(c)], x_ext.at[upper, cols(c)], in_s.at[c], in_r.at[c], (dp, right))

    def mix(c):
        load(cot_hbm, x_cot, ld_cot, c).wait()
        load(gate_hbm, x_gate, ld_gate, c).wait()
        a = x_cot[:, cols(c)].astype(jnp.float32)
        b = x_gate[:, cols(c)].astype(jnp.float32)
        g_ext[upper, cols(c)] = (a * b).astype(jnp.bfloat16)

    each(middle, mix)
    pl.semaphore_wait(barrier, places + ranks)

    def send_rim(c):
        @pl.when(ctx > 0)
        def _():
            rim(c).start()

    each(middle, send_rim)

    @pl.when(jnp.logical_not(last))
    def _():
        each(CHUNKS, lambda c: lend(c).start(), middle)

    each(CHUNKS, lambda c: (mix(c), send_rim(c)), middle)

    def shard(p, s, c):
        return taps_all.at[4 * p + 2 * s + c]

    def tap(p, s, c, sem, to):
        return remote(shard(p, s, c), shard(p, s, c), sem, tap_r.at[4 * p + 2 * s + c], (to, ctx))

    def tap_z(k):
        return tap(place, side, core, tz_s.at[k], z_device(k))

    def tap_y(p):
        return tap(p, side, core, ty_s.at[p], across)

    def tap_c(p, s):
        return tap(p, s, core, tc_s.at[p, s], partner)

    def tap_wait(p, s, c):
        tap(p, s, c, ty_s.at[p], partner).wait_recv()

    own_taps.wait()
    each(places, lambda k: tap_z(k).start(), 1)
    tap_y(place).start()
    tap_c(place, side).start()

    def pass_y():
        def one(k):
            tap_wait(z_peer(k), side, core)
            tap_y(z_peer(k)).start()
            tap_c(z_peer(k), side).start()

        each(places, one, 1)

    def pass_c():
        def one(p):
            tap_wait(p, 1 - side, core)
            tap_c(p, 1 - side).start()

        each(places, one)

    def all_taps():
        def one(p):
            tap_wait(p, 0, 1 - core)
            tap_wait(p, 1, 1 - core)

        each(places, one)

    @pl.when(last)
    def _():
        g_ext[lower, :] = jnp.zeros((rows, channels), jnp.bfloat16)

    @pl.when(first)
    def _():
        x_ext[upper, :] = jnp.zeros((rows, channels), jnp.bfloat16)

    load_f.wait()
    load_b.wait()

    def ahead(x):
        n = x.shape[0]
        return dot(f_all[0, :, :n], x) + dot(f_all[1, :, :n], x)

    def later(x):
        return dot(f_all[0, :, rows:], x) + dot(f_all[1, :, rows:], x)

    def back(value, n):
        high = value.astype(jnp.bfloat16)
        low = (value - high.astype(jnp.float32)).astype(jnp.bfloat16)
        return dot(b_all[0, :n, :], high) + dot(b_all[1, :n, :], high) + dot(b_all[0, :n, :], low)

    half = f_all.shape[1] // 2

    def correlate(a, g, n):
        ar, ai, gr, gi = a[:half], a[half:], g[:half], g[half:]
        return back(jnp.concatenate([ar * gr + ai * gi, ar * gi - ai * gr], 0), n)

    count = taps_all.shape[1]
    taps = 2 * pairs * count
    f32, bf = jnp.float32, jnp.bfloat16

    def chunk(i):
        return jnp.where(last, i, lax.rem(i + middle, CHUNKS))

    def cross(c):
        return remote(csrc.at[:, :, cols(c)], cbuf.at[:, :, cols(c)], c_s.at[c], c_r.at[c], (partner, ctx))

    def turn(c):
        return remote(ysrc.at[:, :, cols(c)], ybuf.at[:, :, cols(c)], y_s.at[c], y_r.at[c], (across, ctx))

    def spread(c, k):
        return remote(
            zsrc.at[z_peer(k), :, cols(c)], zbuf.at[place, :, cols(c)],
            z_s.at[k, c], z_r.at[place, c], (z_device(k), ctx),
        )

    def gathered(c, k):
        slot = zbuf.at[z_peer(k), :, cols(c)]
        return remote(slot, slot, z_s.at[k, c], z_r.at[z_peer(k), c], (z_device(k), ctx))

    def swap(c, k):
        slot = xbuf.at[ctx, :, cols(c)]
        return remote(slot, slot, x_s.at[k, c], x_r.at[ctx, c], (dp, rank(k)))

    def swapped(c, k):
        slot = xbuf.at[rank(k), :, cols(c)]
        return remote(slot, slot, x_s.at[k, c], x_r.at[rank(k), c], (dp, rank(k)))

    def stage1(c):
        load_in(c).wait()

        @pl.when(c < middle)
        def _():
            @pl.when(jnp.logical_not(last))
            def _():
                rim(c).wait_recv()

            p = correlate(ahead(x_ext[lower, cols(c)]), ahead(g_ext[:, cols(c)]), taps)
            p32[...] = p.reshape(places, 2, 2, count, wide)

        @pl.when(c >= middle)
        def _():
            @pl.when(jnp.logical_not(first))
            def _():
                lend(c).wait_recv()

            p = correlate(ahead(x_ext[:, cols(c)]), later(g_ext[upper, cols(c)]), taps)
            p32[...] = p.reshape(places, 2, 2, count, wide)

        for s in range(2):
            csrc[pl.ds(s * places, places), :, cols(c)] = p32[:, s, 1 - core].astype(bf)
            own32[pl.ds(s * places, places), :, cols(c)] = p32[:, s, core]
        cross(c).start()

    def stage2(c):
        cross(c).wait_recv()
        there, here = pl.ds((1 - side) * places, places), pl.ds(side * places, places)
        ysrc[:, :, cols(c)] = (own32[there, :, cols(c)] + cbuf[there, :, cols(c)].astype(f32)).astype(bf)
        turn(c).start()
        half32[:, :, cols(c)] = own32[here, :, cols(c)] + cbuf[here, :, cols(c)].astype(f32)

    def stage3(c):
        turn(c).wait_recv()
        total = half32[:, :, cols(c)] + ybuf[:, :, cols(c)].astype(f32)
        half32[:, :, cols(c)] = total
        zsrc[:, :, cols(c)] = total.astype(bf)
        for k in range(1, places):
            spread(c, k).start()

    def stage4(c):
        total = half32[place, :, cols(c)]
        for k in range(1, places):
            gathered(c, k).wait_recv()
            total = total + zbuf[z_peer(k), :, cols(c)].astype(f32)
        xbuf[ctx, :, cols(c)] = total.astype(bf)
        for k in range(1, ranks):
            swap(c, k).start()

    def finish(c):
        for k in range(1, ranks):
            swapped(c, k).wait_recv()
        total = xbuf[0, :, cols(c)].astype(f32)
        for r in range(1, ranks):
            total = total + xbuf[r, :, cols(c)].astype(f32)
        fbuf[:, cols(c)] = total * scale

    def grad(c):
        @pl.when(jnp.logical_and(c >= middle, jnp.logical_not(last)))
        def _():
            rim(c).wait_recv()

        t = taps_all[:, :, cols(c)].astype(f32).reshape(taps, wide).astype(bf)
        obuf[:, cols(c)] = correlate(ahead(t), ahead(g_ext[:, cols(c)]), rows).astype(bf)

    def step(i):
        for lag, stage in list(zip((0, 1, 3, 5), (stage1, stage2, stage3, stage4))):
            @pl.when(jnp.logical_and(i >= lag, i < CHUNKS + lag))
            def _(lag=lag, stage=stage):
                stage(chunk(i - lag))

        for when, action in ((2, pass_y), (middle + 1, pass_c), (CHUNKS - 1, all_taps)):
            @pl.when(i == when)
            def _(action=action):
                action()

        @pl.when(i >= CHUNKS - 1)
        def _():
            grad(i - CHUNKS + 1)

        @pl.when(i == 2 * CHUNKS - 2)
        def _():
            each(CHUNKS, finish)

    each(2 * CHUNKS - 1, step)

    def drain(c):
        cross(c).wait_send()
        turn(c).wait_send()
        for k in range(1, places):
            spread(c, k).wait_send()
        for k in range(1, ranks):
            swap(c, k).wait_send()

        @pl.when(ctx > 0)
        def _():
            rim(c).wait_send()

    each(CHUNKS, drain)

    @pl.when(jnp.logical_not(last))
    def _():
        each(CHUNKS, lambda c: lend(c).wait_send(), middle)

    each(places, lambda k: tap_z(k).wait_send(), 1)

    def drain_taps(p):
        tap_y(p).wait_send()
        tap_c(p, 0).wait_send()
        tap_c(p, 1).wait_send()

    each(places, drain_taps)


def shards(conv_input, gate_value, out_grad, filter_taps):
    _, rows, channels = conv_input.shape
    count = filter_taps.shape[0]
    members, ranks = lax.axis_size("dp"), lax.axis_size("ctx")
    taps = count * members
    wide = channels // CHUNKS
    if count % 8 or taps != rows or rows % 16 or members % 4 or channels % (128 * CHUNKS):
        return general(conv_input, gate_value, out_grad, filter_taps)
    pairs = members // 2
    places = pairs // 2
    scale = 1.0 / math.sqrt(rows * ranks * members)
    forward, inverse = transforms(rows + taps)
    hbm = pl.BlockSpec(memory_space=pltpu.HBM)
    bf, f32, dma, vmem = jnp.bfloat16, jnp.float32, pltpu.SemaphoreType.DMA, pltpu.VMEM
    out, fgrad = pl.pallas_call(
        functools.partial(kernel, pairs, ranks, scale),
        out_shape=(
            vmem((rows, channels), bf),
            vmem((count, channels), f32),
        ),
        in_specs=[hbm] * 6,
        out_specs=(pl.BlockSpec(memory_space=vmem),) * 2,
        scratch_shapes=[
            vmem((rows, channels), bf),
            vmem((rows, channels), bf),
            vmem((2 * rows, channels), bf),
            vmem((2 * rows, channels), bf),
            vmem((members, count, channels), bf),
            vmem((2, rows + taps, rows + taps), bf),
            vmem((2, rows + taps, rows + taps), bf),
            vmem((places, 2, 2, count, wide), f32),
            vmem((pairs, count, channels), f32),
            vmem((pairs, count, channels), bf),
            vmem((pairs, count, channels), bf),
            vmem((places, count, channels), f32),
            vmem((places, count, channels), bf),
            vmem((places, count, channels), bf),
            vmem((places, count, channels), bf),
            vmem((places, count, channels), bf),
            vmem((ranks, count, channels), bf),
            dma((CHUNKS,)), dma((CHUNKS,)), dma((CHUNKS,)), dma, dma((2,)),
            dma((CHUNKS,)), dma((CHUNKS,)), dma((CHUNKS,)), dma((CHUNKS,)),
            dma((places,)), dma((places,)), dma((places, 2)), dma((members,)),
            dma((CHUNKS,)), dma((CHUNKS,)), dma((CHUNKS,)), dma((CHUNKS,)),
            dma((places, CHUNKS)), dma((places, CHUNKS)),
            dma((ranks, CHUNKS)), dma((ranks, CHUNKS)),
        ],
        compiler_params=pltpu.CompilerParams(
            collective_id=0, has_side_effects=True, vmem_limit_bytes=40_000_000
        ),
    )(*(
        pltpu.with_memory_space_constraint(x, pltpu.HBM)
        for x in (conv_input[0], gate_value[0], out_grad[0], filter_taps, jnp.asarray(np.stack(forward)), jnp.asarray(np.stack(inverse)))
    ))
    return store(out, fgrad)


PARTS = 8


def store(grad, fgrad):
    rows, channels = grad.shape
    wide = channels // PARTS

    def body(g_ref, f_ref, g_out, f_out, sems):
        def copies():
            for k in range(PARTS):
                at = pl.ds(k * (rows // PARTS), rows // PARTS)
                yield pltpu.make_async_copy(g_ref.at[at], g_out.at[0, at], sems.at[k])
            yield pltpu.make_async_copy(f_ref, f_out, sems.at[PARTS])

        for copy in copies():
            copy.start()
        for copy in copies():
            copy.wait()

    return pl.pallas_call(
        body,
        out_shape=(
            jax.ShapeDtypeStruct((1, rows, channels), grad.dtype),
            jax.ShapeDtypeStruct(fgrad.shape, fgrad.dtype),
        ),
        in_specs=[pl.BlockSpec(memory_space=pltpu.VMEM)] * 2,
        out_specs=(pl.BlockSpec(memory_space=pl.ANY),) * 2,
        scratch_shapes=[pltpu.SemaphoreType.DMA((PARTS + 1,))],
    )(pltpu.with_memory_space_constraint(grad, pltpu.VMEM), pltpu.with_memory_space_constraint(fgrad, pltpu.VMEM))


def solution(mesh):
    in_specs = (P("dp", "ctx", None), P("dp", "ctx", None), P("dp", "ctx", None), P("dp", None))
    out_specs = (P("dp", "ctx", None), P("dp", None))
    return jax.shard_map(shards, mesh=mesh, in_specs=in_specs, out_specs=out_specs, check_vma=False)
```

```python
import functools
import math

import jax
import jax.numpy as jnp
import numpy as np
from jax import lax
from jax.experimental import pallas as pl
from jax.experimental.pallas import tpu as pltpu
from jax.sharding import PartitionSpec as P


def split(values):
    high = values.astype(jnp.bfloat16)
    return high, (values - high.astype(np.float32)).astype(jnp.bfloat16)


def transforms(length):
    half = length // 2
    angle = np.pi * np.outer(2 * np.arange(half) + 1, np.arange(length)) / length
    forward = np.concatenate([np.cos(angle), -np.sin(angle)], 0)
    inverse = np.concatenate([np.cos(angle), -np.sin(angle)], 0).T / half
    return split(forward.astype(np.float32)), split(inverse.astype(np.float32))


def dot(a, b):
    return lax.dot_general(a, b, (((1,), (0,)), ((), ())), preferred_element_type=jnp.float32)


def general(conv_input, gate_value, out_grad, filter_taps):
    inputs = conv_input[0]
    rows = inputs.shape[0]
    taps = filter_taps.shape[0] * lax.axis_size("dp")
    (fh, fl), (bh, bl) = transforms(rows + taps)
    half = (rows + taps) // 2
    mixed = (out_grad[0].astype(jnp.float32) * gate_value[0].astype(jnp.float32)).astype(
        jnp.bfloat16
    )
    devices = lax.axis_size("ctx")
    rim = lax.ppermute(mixed[:taps], "ctx", [(i + 1, i) for i in range(devices - 1)])
    full_taps = lax.all_gather(filter_taps, "dp", axis=0, tiled=True)

    def spectrum(x, first=0):
        n = x.shape[0]
        s = dot(fh[:, first : first + n], x) + dot(fl[:, first : first + n], x)
        return s[:half], s[half:]

    def back(re, im, n):
        s = jnp.concatenate([re, im], 0)
        high = s.astype(jnp.bfloat16)
        low = (s - high.astype(jnp.float32)).astype(jnp.bfloat16)
        return dot(bh[:n], high) + dot(bl[:n], high) + dot(bh[:n], low)

    xr, xi = spectrum(inputs)
    gr0, gi0 = spectrum(mixed)
    gr1, gi1 = spectrum(rim, rows)
    gr, gi = gr0 + gr1, gi0 + gi1
    partial = back(xr * gr + xi * gi, xr * gi - xi * gr, taps)
    hr, hi = spectrum(full_taps)
    grad = back(hr * gr + hi * gi, hr * gi - hi * gr, rows)
    shard_grad = lax.psum(lax.psum_scatter(partial, "dp", scatter_dimension=0, tiled=True), "ctx")
    tokens_all = rows * devices * lax.axis_size("dp")
    return (grad.astype(jnp.bfloat16)[None], shard_grad * (1.0 / math.sqrt(tokens_all)))


CHUNKS = 8
MESH = pl.DeviceIdType.MESH


def kernel(
    pairs, scale,
    in_hbm, gate_hbm, cot_hbm, taps_hbm, f_hbm,
    obuf, fbuf,
    x_gc, x_in, g, inc, taps_all, f_all, xs, gs, hs, p32, own32, csrc, cbuf, half32, ysrc, ybuf,
    zsrc, zbuf, xbuf,
    ld_gc, ld_in, ld_taps, ld_f, met,
    inc_s, inc_r, tz_s, tz_r, ty_s, ty_r, tc_s, tc_r,
    c_s, c_r, y_s, y_r, z_s, z_r, x_s, x_r,
):
    dp, ctx = lax.axis_index("dp"), lax.axis_index("ctx")
    core, mine = lax.rem(dp, 2), dp // 2
    partner = dp + 1 - 2 * core
    side, place, places = lax.rem(mine, 2), mine // 2, pairs // 2
    across = 2 * (mine + 1 - 2 * side) + core
    rows, channels = g.shape
    wide = channels // CHUNKS
    middle = CHUNKS // 2
    first, last = ctx == 0, ctx == 1
    other = 1 - ctx
    f32, bf = jnp.float32, jnp.bfloat16
    count = taps_all.shape[1]
    half = rows

    def cols(c):
        return pl.ds(pl.multiple_of(c * wide, wide), wide)

    def each(n, body, start=0):
        lax.fori_loop(start, n, lambda i, z: (body(i), z)[1], 0)

    def local(src, dst, sem):
        return pltpu.make_async_copy(src, dst, sem)

    def remote(src, dst, send, recv, to):
        return pltpu.make_async_remote_copy(
            src_ref=src, dst_ref=dst, send_sem=send, recv_sem=recv, device_id=to, device_id_type=MESH
        )

    own_taps = local(taps_hbm, taps_all.at[dp], ld_taps)
    load_f = local(f_hbm, f_all, ld_f)
    load_in = local(in_hbm, x_in, ld_in)

    def loads(c):
        local(cot_hbm.at[:, cols(c)], x_gc.at[0, :, cols(c)], ld_gc.at[c]).start()
        local(gate_hbm.at[:, cols(c)], x_gc.at[1, :, cols(c)], ld_gc.at[c]).start()

    each(CHUNKS, loads)

    barrier = pltpu.get_barrier_semaphore()

    @pl.when(first)
    def _():
        pl.semaphore_signal(barrier, inc=1, device_id=(dp, other), device_id_type=MESH)

    own_taps.start()
    load_f.start()
    load_in.start()

    @pl.when(last)
    def _():
        pl.semaphore_wait(barrier, 1)
        pl.semaphore_signal(met, inc=1, device_id=(dp, other), device_id_type=MESH)

    def z_peer(k):
        return lax.rem(place + k, places)

    def z_device(k):
        return 4 * z_peer(k) + 2 * side + core

    def rim(c):
        return remote(g.at[:, cols(c)], inc.at[:, cols(c)], inc_s, inc_r.at[c], (dp, other))

    def lend(c):
        return remote(in_hbm.at[:, cols(c)], inc.at[:, cols(c)], inc_s, inc_r.at[c], (dp, other))

    def mix(c):
        both = x_gc.at[:, :, cols(c)]
        local(both, both, ld_gc.at[c]).wait()
        a = x_gc[0, :, cols(c)].astype(f32)
        b = x_gc[1, :, cols(c)].astype(f32)
        g[:, cols(c)] = (a * b).astype(bf)

        @pl.when(last)
        def _():
            rim(c).start()

    each(CHUNKS, mix)

    @pl.when(first)
    def _():
        pl.semaphore_wait(met, 1)
        pl.semaphore_signal(barrier, inc=1, device_id=(partner, ctx), device_id_type=MESH)
        pl.semaphore_signal(barrier, inc=1, device_id=(across, ctx), device_id_type=MESH)
        for k in range(1, places):
            pl.semaphore_signal(barrier, inc=1, device_id=(z_device(k), ctx), device_id_type=MESH)
        each(CHUNKS, lambda c: lend(c).start(), middle)

    def ahead(which, x):
        return jnp.dot(f_all[which], jnp.concatenate([x, x], 0), preferred_element_type=f32)

    def correlate(a, b):
        ar, ai, br, bi = a[:half], a[half:], b[:half], b[half:]
        value = jnp.concatenate([ar * br + ai * bi, ar * bi - ai * br], 0)
        high = value.astype(bf)
        low = (value - high.astype(f32)).astype(bf)
        both = jnp.dot(f_all[2], high, preferred_element_type=f32)
        return both[:half] + both[half:] + jnp.dot(f_all[2, :half, :], low, preferred_element_type=f32)

    def chunk(i):
        return jnp.where(last, i, lax.rem(i + middle, CHUNKS))

    def emit(a, b, c):
        p32[...] = correlate(a, b).reshape(places, 2, 2, count, wide)
        for s in range(2):
            csrc[pl.ds(s * places, places), :, cols(c)] = p32[:, s, 1 - core].astype(bf)
            own32[pl.ds(s * places, places), :, cols(c)] = p32[:, s, core]

    def front(i):
        c = chunk(i)
        a, b = ahead(0, x_in[:, cols(c)]), ahead(0, g[:, cols(c)])
        gs[:, cols(c)] = b

        @pl.when(i < middle)
        def _():
            emit(a, b, c)

        @pl.when(i >= middle)
        def _():
            xs[:, cols(c)] = a

    load_f.wait()
    load_in.wait()
    each(CHUNKS, front)

    @pl.when(first)
    def _():
        pl.semaphore_wait(barrier, places + 1)
        pl.semaphore_signal(met, inc=1, device_id=(dp, other), device_id_type=MESH)

    @pl.when(last)
    def _():
        pl.semaphore_wait(met, 1)

    def shard(p, s, c):
        return taps_all.at[4 * p + 2 * s + c]

    def tap_z(k):
        return remote(shard(place, side, core), shard(place, side, core), tz_s, tz_r.at[place], (z_device(k), ctx))

    def tap_y(p):
        return remote(shard(p, side, core), shard(p, side, core), ty_s, ty_r.at[p], (across, ctx))

    def tap_c(p, s):
        return remote(shard(p, s, core), shard(p, s, core), tc_s, tc_r, (partner, ctx))

    def tap_wait(p, s, sem):
        remote(shard(p, s, core), shard(p, s, core), tz_s, sem, (partner, ctx)).wait_recv()

    def pass_y(k):
        p = z_peer(k)
        tap_wait(p, side, tz_r.at[p])
        tap_y(p).start()
        tap_c(p, side).start()

    def pass_c(p):
        tap_wait(p, 1 - side, ty_r.at[p])
        tap_c(p, 1 - side).start()

    def cross(c):
        return remote(csrc.at[:, :, cols(c)], cbuf.at[:, :, cols(c)], c_s, c_r.at[c], (partner, ctx))

    def turn(c):
        return remote(ysrc.at[:, :, cols(c)], ybuf.at[:, :, cols(c)], y_s, y_r.at[c], (across, ctx))

    def spread(c, k):
        return remote(
            zsrc.at[z_peer(k), :, cols(c)], zbuf.at[place, :, cols(c)], z_s, z_r.at[c], (z_device(k), ctx)
        )

    def gathered(c):
        slots = zbuf.at[pl.ds(0, places - 1), :, cols(c)]
        return remote(slots, slots, z_s, z_r.at[c], (z_device(1), ctx))

    def swap(c):
        slot = xbuf.at[ctx, :, cols(c)]
        return remote(slot, slot, x_s, x_r, (dp, other))

    def stage2(i):
        c = chunk(i)
        cross(c).wait_recv()
        there, here = pl.ds((1 - side) * places, places), pl.ds(side * places, places)
        ysrc[:, :, cols(c)] = (own32[there, :, cols(c)] + cbuf[there, :, cols(c)].astype(f32)).astype(bf)
        turn(c).start()
        half32[:, :, cols(c)] = own32[here, :, cols(c)] + cbuf[here, :, cols(c)].astype(f32)

    def stage3(i):
        c = chunk(i)
        turn(c).wait_recv()
        total = half32[:, :, cols(c)] + ybuf[:, :, cols(c)].astype(f32)
        half32[:, :, cols(c)] = total
        zsrc[:, :, cols(c)] = total.astype(bf)
        for k in range(1, places):
            spread(c, k).start()

    def stage4(i):
        c = chunk(i)
        gathered(c).wait_recv()
        total = half32[place, :, cols(c)]
        for k in range(1, places):
            total = total + zbuf[z_peer(k), :, cols(c)].astype(f32)
        xbuf[ctx, :, cols(c)] = total.astype(bf)
        swap(c).start()

    keep, drop = other.astype(f32), ctx.astype(f32)

    def arrive(c):
        remote(inc.at[:, cols(c)], inc.at[:, cols(c)], inc_s, inc_r.at[c], (dp, other)).wait_recv()
        return ahead(1, inc[:, cols(c)])

    def meet(i):
        c = chunk(i)
        w = arrive(c)
        b = gs[:, cols(c)] + keep * w
        gs[:, cols(c)] = b
        emit(xs[:, cols(c)] - drop * w, b, c)
        cross(c).start()

    def spectrum(c):
        t = taps_all[:, :, cols(c)].astype(f32).reshape(rows, wide).astype(bf)
        hs[:, cols(c)] = ahead(0, t)

    def grad(c):
        @pl.when(jnp.logical_and(first, c >= middle))
        def _():
            gs[:, cols(c)] += arrive(c)

        obuf[:, cols(c)] = correlate(hs[:, cols(c)], gs[:, cols(c)]).astype(bf)

    own_taps.wait()
    each(places, lambda k: tap_z(k).start(), 1)
    tap_y(place).start()
    tap_c(place, side).start()
    each(middle, lambda i: cross(chunk(i)).start())

    def at(i, when, action):
        @pl.when(i == when)
        def _():
            action()

    def follow(i):
        meet(i)
        at(i, middle, lambda: each(middle, stage2))
        at(i, middle + 1, lambda: each(middle, stage3))
        at(i, middle + 1, lambda: pass_y(1))

        @pl.when(i > middle)
        def _():
            stage2(i - 1)

        @pl.when(i > middle + 1)
        def _():
            stage3(i - 2)

        at(i, middle + 2, lambda: each(places, pass_y, 2))
        at(i, middle + 3, lambda: each(middle, stage4))

    each(CHUNKS, follow, middle)

    each(places, pass_c)
    theirs = taps_all.at[pl.ds(0, pairs)]
    remote(theirs, theirs, tc_s, tc_r, (partner, ctx)).wait_recv()
    each(CHUNKS, spectrum)

    def slot(c):
        grad(c)
        at(c, 1, lambda: stage2(CHUNKS - 1))
        at(c, 2, lambda: stage3(CHUNKS - 2))
        at(c, 3, lambda: stage4(middle))
        at(c, 4, lambda: stage3(CHUNKS - 1))
        at(c, 5, lambda: each(CHUNKS - 1, stage4, middle + 1))
        at(c, 6, lambda: stage4(CHUNKS - 1))

    each(CHUNKS, slot)

    theirs = xbuf.at[other]
    remote(theirs, theirs, x_s, x_r, (dp, other)).wait_recv()
    fbuf[...] = (xbuf[0].astype(f32) + xbuf[1].astype(f32)) * scale

    def sent(ref, sem):
        remote(ref, ref, sem, x_r, (dp, other)).wait_send()

    sent(csrc, c_s)
    sent(ysrc, y_s)
    sent(zsrc.at[pl.ds(0, places - 1)], z_s)
    sent(xbuf.at[ctx], x_s)
    sent(taps_all.at[pl.ds(0, places - 1)], tz_s)
    sent(taps_all.at[pl.ds(0, places)], ty_s)
    sent(taps_all.at[pl.ds(0, pairs)], tc_s)

    @pl.when(last)
    def _():
        sent(g, inc_s)

    @pl.when(first)
    def _():
        sent(g.at[:, pl.ds(0, channels // 2)], inc_s)


def shards(conv_input, gate_value, out_grad, filter_taps):
    _, rows, channels = conv_input.shape
    count = filter_taps.shape[0]
    members, ranks = lax.axis_size("dp"), lax.axis_size("ctx")
    taps = count * members
    wide = channels // CHUNKS
    if ranks != 2 or count % 8 or taps != rows or rows % 16 or members % 4 or channels % (128 * CHUNKS):
        return general(conv_input, gate_value, out_grad, filter_taps)
    pairs = members // 2
    places = pairs // 2
    scale = 1.0 / math.sqrt(rows * ranks * members)
    (fh, fl), (bh, bl) = transforms(rows + taps)
    matrices = np.stack([
        np.concatenate([fh[:, :rows], fl[:, :rows]], 1),
        np.concatenate([fh[:, rows:], fl[:, rows:]], 1),
        np.concatenate([bh[:rows], bl[:rows]], 0),
    ])
    hbm = pl.BlockSpec(memory_space=pltpu.HBM)
    bf, f32, dma, vmem = jnp.bfloat16, jnp.float32, pltpu.SemaphoreType.DMA, pltpu.VMEM
    out, fgrad = pl.pallas_call(
        functools.partial(kernel, pairs, scale),
        out_shape=(vmem((rows, channels), bf), vmem((count, channels), f32)),
        in_specs=[hbm] * 5,
        out_specs=(pl.BlockSpec(memory_space=vmem),) * 2,
        scratch_shapes=[
            vmem((2, rows, channels), bf),
            vmem((rows, channels), bf),
            vmem((rows, channels), bf),
            vmem((rows, channels), bf),
            vmem((members, count, channels), bf),
            vmem((3, rows + taps, rows + taps), bf),
            vmem((rows + taps, channels), f32),
            vmem((rows + taps, channels), f32),
            vmem((rows + taps, channels), f32),
            vmem((places, 2, 2, count, wide), f32),
            vmem((pairs, count, channels), f32),
            vmem((pairs, count, channels), bf),
            vmem((pairs, count, channels), bf),
            vmem((places, count, channels), f32),
            vmem((places, count, channels), bf),
            vmem((places, count, channels), bf),
            vmem((places, count, channels), bf),
            vmem((places, count, channels), bf),
            vmem((ranks, count, channels), bf),
            dma((CHUNKS,)), dma, dma, dma, pltpu.SemaphoreType.REGULAR,
            dma, dma((CHUNKS,)), dma, dma((places,)), dma, dma((places,)), dma, dma,
            dma, dma((CHUNKS,)), dma, dma((CHUNKS,)), dma, dma((CHUNKS,)), dma, dma,
        ],
        compiler_params=pltpu.CompilerParams(
            collective_id=0, has_side_effects=True, vmem_limit_bytes=48_000_000
        ),
    )(*(
        pltpu.with_memory_space_constraint(x, pltpu.HBM)
        for x in (conv_input[0], gate_value[0], out_grad[0], filter_taps, jnp.asarray(matrices))
    ))
    return store(out, fgrad)


PARTS = 8


def store(grad, fgrad):
    rows, channels = grad.shape
    wide = channels // PARTS

    def body(g_ref, f_ref, g_out, f_out, sems):
        def copies():
            for k in range(PARTS):
                at = pl.ds(k * (rows // PARTS), rows // PARTS)
                yield pltpu.make_async_copy(g_ref.at[at], g_out.at[0, at], sems.at[k])
            yield pltpu.make_async_copy(f_ref, f_out, sems.at[PARTS])

        for copy in copies():
            copy.start()
        for copy in copies():
            copy.wait()

    return pl.pallas_call(
        body,
        out_shape=(
            jax.ShapeDtypeStruct((1, rows, channels), grad.dtype),
            jax.ShapeDtypeStruct(fgrad.shape, fgrad.dtype),
        ),
        in_specs=[pl.BlockSpec(memory_space=pltpu.VMEM)] * 2,
        out_specs=(pl.BlockSpec(memory_space=pl.ANY),) * 2,
        scratch_shapes=[pltpu.SemaphoreType.DMA((PARTS + 1,))],
    )(pltpu.with_memory_space_constraint(grad, pltpu.VMEM), pltpu.with_memory_space_constraint(fgrad, pltpu.VMEM))


def solution(mesh):
    in_specs = (P("dp", "ctx", None), P("dp", "ctx", None), P("dp", "ctx", None), P("dp", None))
    out_specs = (P("dp", "ctx", None), P("dp", None))
    return jax.shard_map(shards, mesh=mesh, in_specs=in_specs, out_specs=out_specs, check_vma=False)
```

```python
import functools
import math

import jax
import jax.numpy as jnp
import numpy as np
from jax import lax
from jax.experimental import pallas as pl
from jax.experimental.pallas import tpu as pltpu
from jax.sharding import PartitionSpec as P


def split(values):
    high = values.astype(jnp.bfloat16)
    return high, (values - high.astype(np.float32)).astype(jnp.bfloat16)


def transforms(length):
    half = length // 2
    angle = np.pi * np.outer(2 * np.arange(half) + 1, np.arange(length)) / length
    forward = np.concatenate([np.cos(angle), -np.sin(angle)], 0)
    inverse = np.concatenate([np.cos(angle), -np.sin(angle)], 0).T / half
    return split(forward.astype(np.float32)), split(inverse.astype(np.float32))


def dot(a, b):
    return lax.dot_general(a, b, (((1,), (0,)), ((), ())), preferred_element_type=jnp.float32)


def general(conv_input, gate_value, out_grad, filter_taps):
    inputs = conv_input[0]
    rows = inputs.shape[0]
    taps = filter_taps.shape[0] * lax.axis_size("dp")
    (fh, fl), (bh, bl) = transforms(rows + taps)
    half = (rows + taps) // 2
    mixed = (out_grad[0].astype(jnp.float32) * gate_value[0].astype(jnp.float32)).astype(
        jnp.bfloat16
    )
    devices = lax.axis_size("ctx")
    rim = lax.ppermute(mixed[:taps], "ctx", [(i + 1, i) for i in range(devices - 1)])
    full_taps = lax.all_gather(filter_taps, "dp", axis=0, tiled=True)

    def spectrum(x, first=0):
        n = x.shape[0]
        s = dot(fh[:, first : first + n], x) + dot(fl[:, first : first + n], x)
        return s[:half], s[half:]

    def back(re, im, n):
        s = jnp.concatenate([re, im], 0)
        high = s.astype(jnp.bfloat16)
        low = (s - high.astype(jnp.float32)).astype(jnp.bfloat16)
        return dot(bh[:n], high) + dot(bl[:n], high) + dot(bh[:n], low)

    xr, xi = spectrum(inputs)
    gr0, gi0 = spectrum(mixed)
    gr1, gi1 = spectrum(rim, rows)
    gr, gi = gr0 + gr1, gi0 + gi1
    partial = back(xr * gr + xi * gi, xr * gi - xi * gr, taps)
    hr, hi = spectrum(full_taps)
    grad = back(hr * gr + hi * gi, hr * gi - hi * gr, rows)
    shard_grad = lax.psum(lax.psum_scatter(partial, "dp", scatter_dimension=0, tiled=True), "ctx")
    tokens_all = rows * devices * lax.axis_size("dp")
    return (grad.astype(jnp.bfloat16)[None], shard_grad * (1.0 / math.sqrt(tokens_all)))


CHUNKS = 8
EARLY = 2
LATE = 4
MESH = pl.DeviceIdType.MESH


def kernel(
    pairs, scale,
    in_hbm, gate_hbm, cot_hbm, taps_hbm, f_hbm,
    obuf, fbuf,
    x_gc, x_in, g, inc, taps_all, f_all, xs, gs, hs, p32, own32, csrc, cbuf, half32, ysrc, ybuf,
    zsrc, zbuf, xbuf,
    ld_gc, ld_in, ld_taps, ld_f, met,
    inc_s, inc_r, tz_s, tz_r, ty_s, ty_r, tc_s, tc_r,
    c_s, c_r, y_s, y_r, z_s, z_r, x_s, x_r,
):
    dp, ctx = lax.axis_index("dp"), lax.axis_index("ctx")
    core, mine = lax.rem(dp, 2), dp // 2
    partner = dp + 1 - 2 * core
    side, place, places = lax.rem(mine, 2), mine // 2, pairs // 2
    across = 2 * (mine + 1 - 2 * side) + core
    rows, channels = g.shape
    wide = channels // CHUNKS
    middle = CHUNKS // 2
    first, last = ctx == 0, ctx == 1
    other = 1 - ctx
    f32, bf = jnp.float32, jnp.bfloat16
    count = taps_all.shape[1]
    half = rows

    def cols(c):
        return pl.ds(pl.multiple_of(c * wide, wide), wide)

    def each(n, body, start=0):
        lax.fori_loop(start, n, lambda i, z: (body(i), z)[1], 0)

    def local(src, dst, sem):
        return pltpu.make_async_copy(src, dst, sem)

    def remote(src, dst, send, recv, to):
        return pltpu.make_async_remote_copy(
            src_ref=src, dst_ref=dst, send_sem=send, recv_sem=recv, device_id=to, device_id_type=MESH
        )

    own_taps = local(taps_hbm, taps_all.at[dp], ld_taps)
    load_f = local(f_hbm, f_all, ld_f)
    load_in = local(in_hbm, x_in, ld_in)

    def loads(c):
        local(cot_hbm.at[:, cols(c)], x_gc.at[0, :, cols(c)], ld_gc.at[c]).start()
        local(gate_hbm.at[:, cols(c)], x_gc.at[1, :, cols(c)], ld_gc.at[c]).start()

    each(CHUNKS, loads)

    barrier = pltpu.get_barrier_semaphore()

    @pl.when(first)
    def _():
        pl.semaphore_signal(barrier, inc=1, device_id=(dp, other), device_id_type=MESH)

    own_taps.start()
    load_f.start()
    load_in.start()

    @pl.when(last)
    def _():
        pl.semaphore_wait(barrier, 1)
        pl.semaphore_signal(met, inc=1, device_id=(dp, other), device_id_type=MESH)

    def z_peer(k):
        return lax.rem(place + k, places)

    def z_device(k):
        return 4 * z_peer(k) + 2 * side + core

    def rim(c):
        return remote(g.at[:, cols(c)], inc.at[:, cols(c)], inc_s, inc_r.at[c], (dp, other))

    def lend(c):
        return remote(in_hbm.at[:, cols(c)], inc.at[:, cols(c)], inc_s, inc_r.at[c], (dp, other))

    def mix(c):
        both = x_gc.at[:, :, cols(c)]
        local(both, both, ld_gc.at[c]).wait()
        a = x_gc[0, :, cols(c)].astype(f32)
        b = x_gc[1, :, cols(c)].astype(f32)
        g[:, cols(c)] = (a * b).astype(bf)

        @pl.when(last)
        def _():
            rim(c).start()

    each(CHUNKS, mix)

    @pl.when(first)
    def _():
        pl.semaphore_wait(met, 1)
        pl.semaphore_signal(barrier, inc=1, device_id=(partner, ctx), device_id_type=MESH)
        pl.semaphore_signal(barrier, inc=1, device_id=(across, ctx), device_id_type=MESH)
        for k in range(1, places):
            pl.semaphore_signal(barrier, inc=1, device_id=(z_device(k), ctx), device_id_type=MESH)
        each(CHUNKS, lambda c: lend(c).start(), middle)

    def ahead(which, x):
        return jnp.dot(f_all[which], jnp.concatenate([x, x], 0), preferred_element_type=f32)

    def correlate(a, b):
        ar, ai, br, bi = a[:half], a[half:], b[:half], b[half:]
        value = jnp.concatenate([ar * br + ai * bi, ar * bi - ai * br], 0)
        high = value.astype(bf)
        low = (value - high.astype(f32)).astype(bf)
        both = jnp.dot(f_all[2], high, preferred_element_type=f32)
        return both[:half] + both[half:] + jnp.dot(f_all[2, :half, :], low, preferred_element_type=f32)

    def chunk(i):
        return jnp.where(last, i, lax.rem(i + middle, CHUNKS))

    def emit(a, b, c):
        p32[...] = correlate(a, b).reshape(places, 2, 2, count, wide)
        for s in range(2):
            csrc[pl.ds(s * places, places), :, cols(c)] = p32[:, s, 1 - core].astype(bf)
            own32[pl.ds(s * places, places), :, cols(c)] = p32[:, s, core]

    def front(i):
        c = chunk(i)
        a, b = ahead(0, x_in[:, cols(c)]), ahead(0, g[:, cols(c)])
        gs[:, cols(c)] = b

        @pl.when(i < middle)
        def _():
            emit(a, b, c)

        @pl.when(i >= middle)
        def _():
            xs[:, cols(c)] = a

    def shard(p, s, c):
        return taps_all.at[4 * p + 2 * s + c]

    def tap_z(k):
        return remote(shard(place, side, core), shard(place, side, core), tz_s, tz_r.at[place], (z_device(k), ctx))

    def tap_y(p):
        return remote(shard(p, side, core), shard(p, side, core), ty_s, ty_r.at[p], (across, ctx))

    def tap_c(p, s):
        return remote(shard(p, s, core), shard(p, s, core), tc_s, tc_r, (partner, ctx))

    def tap_wait(p, s, sem):
        remote(shard(p, s, core), shard(p, s, core), tz_s, sem, (partner, ctx)).wait_recv()

    def pass_y(k):
        p = z_peer(k)
        tap_wait(p, side, tz_r.at[p])
        tap_y(p).start()
        tap_c(p, side).start()

    def pass_c(p):
        tap_wait(p, 1 - side, ty_r.at[p])
        tap_c(p, 1 - side).start()

    def cross(c):
        return remote(csrc.at[:, :, cols(c)], cbuf.at[:, :, cols(c)], c_s, c_r.at[c], (partner, ctx))

    def turn(c):
        return remote(ysrc.at[:, :, cols(c)], ybuf.at[:, :, cols(c)], y_s, y_r.at[c], (across, ctx))

    def spread(c, k):
        return remote(
            zsrc.at[z_peer(k), :, cols(c)], zbuf.at[place, :, cols(c)], z_s, z_r.at[c], (z_device(k), ctx)
        )

    def gathered(c):
        slots = zbuf.at[pl.ds(0, places - 1), :, cols(c)]
        return remote(slots, slots, z_s, z_r.at[c], (z_device(1), ctx))

    def swap(c):
        slot = xbuf.at[ctx, :, cols(c)]
        return remote(slot, slot, x_s, x_r, (dp, other))

    def stage2(i):
        c = chunk(i)
        cross(c).wait_recv()
        there, here = pl.ds((1 - side) * places, places), pl.ds(side * places, places)
        ysrc[:, :, cols(c)] = (own32[there, :, cols(c)] + cbuf[there, :, cols(c)].astype(f32)).astype(bf)
        turn(c).start()
        half32[:, :, cols(c)] = own32[here, :, cols(c)] + cbuf[here, :, cols(c)].astype(f32)

    def stage3(i):
        c = chunk(i)
        turn(c).wait_recv()
        total = half32[:, :, cols(c)] + ybuf[:, :, cols(c)].astype(f32)
        half32[:, :, cols(c)] = total
        zsrc[:, :, cols(c)] = total.astype(bf)
        for k in range(1, places):
            spread(c, k).start()

    def stage4(i):
        c = chunk(i)
        gathered(c).wait_recv()
        total = half32[place, :, cols(c)]
        for k in range(1, places):
            total = total + zbuf[z_peer(k), :, cols(c)].astype(f32)
        xbuf[ctx, :, cols(c)] = total.astype(bf)
        swap(c).start()

    keep, drop = other.astype(f32), ctx.astype(f32)

    def arrive(c):
        remote(inc.at[:, cols(c)], inc.at[:, cols(c)], inc_s, inc_r.at[c], (dp, other)).wait_recv()
        return ahead(1, inc[:, cols(c)])

    def meet(i):
        c = chunk(i)
        w = arrive(c)
        b = gs[:, cols(c)] + keep * w
        gs[:, cols(c)] = b
        emit(xs[:, cols(c)] - drop * w, b, c)
        cross(c).start()

    def spectrum(c):
        t = taps_all[:, :, cols(c)].astype(f32).reshape(rows, wide).astype(bf)
        hs[:, cols(c)] = ahead(0, t)

    def grad(c):
        @pl.when(jnp.logical_and(first, c >= middle))
        def _():
            gs[:, cols(c)] += arrive(c)

        obuf[:, cols(c)] = correlate(hs[:, cols(c)], gs[:, cols(c)]).astype(bf)

    def at(i, when, *actions):
        @pl.when(i == when)
        def _():
            for action in actions:
                action()

    def meet_plane():
        @pl.when(first)
        def _():
            pl.semaphore_wait(barrier, places + 1)
            pl.semaphore_signal(met, inc=1, device_id=(dp, other), device_id_type=MESH)

        @pl.when(last)
        def _():
            pl.semaphore_wait(met, 1)

        own_taps.wait()
        each(places, lambda k: tap_z(k).start(), 1)
        tap_y(place).start()
        tap_c(place, side).start()
        each(EARLY, lambda i: cross(chunk(i)).start())

    def begin(i):
        front(i)

        @pl.when(jnp.logical_and(i >= EARLY, i < middle))
        def _():
            cross(chunk(i)).start()

        at(i, EARLY - 1, meet_plane)

    load_f.wait()
    load_in.wait()
    each(CHUNKS, begin)
    each(middle, stage2)

    def follow(i):
        meet(i)
        at(i, middle, lambda: pass_y(1))
        at(i, middle + 1, lambda: each(middle, stage3))
        stage2(i)
        at(i, middle + 1, lambda: each(places, pass_y, 2), lambda: stage3(middle))
        at(i, middle + 2, lambda: each(middle, stage4), lambda: stage3(middle + 1))

    each(CHUNKS, follow, middle)

    each(places, pass_c)
    stage4(middle)
    stage3(middle + 2)
    theirs = taps_all.at[pl.ds(0, pairs)]
    remote(theirs, theirs, tc_s, tc_r, (partner, ctx)).wait_recv()

    def spectra(c):
        spectrum(c)
        at(c, middle - 1, lambda: stage4(middle + 1), lambda: stage3(middle + 3))

    each(CHUNKS, spectra)

    def slot(c):
        grad(c)
        at(c, 0, lambda: stage4(middle + 2))
        at(c, LATE, lambda: stage4(middle + 3))

    each(CHUNKS, slot)

    theirs = xbuf.at[other]
    remote(theirs, theirs, x_s, x_r, (dp, other)).wait_recv()
    fbuf[...] = (xbuf[0].astype(f32) + xbuf[1].astype(f32)) * scale

    def sent(ref, sem):
        remote(ref, ref, sem, x_r, (dp, other)).wait_send()

    sent(csrc, c_s)
    sent(ysrc, y_s)
    sent(zsrc.at[pl.ds(0, places - 1)], z_s)
    sent(xbuf.at[ctx], x_s)
    sent(taps_all.at[pl.ds(0, places - 1)], tz_s)
    sent(taps_all.at[pl.ds(0, places)], ty_s)
    sent(taps_all.at[pl.ds(0, pairs)], tc_s)

    @pl.when(last)
    def _():
        sent(g, inc_s)

    @pl.when(first)
    def _():
        sent(g.at[:, pl.ds(0, channels // 2)], inc_s)


def shards(conv_input, gate_value, out_grad, filter_taps):
    _, rows, channels = conv_input.shape
    count = filter_taps.shape[0]
    members, ranks = lax.axis_size("dp"), lax.axis_size("ctx")
    taps = count * members
    wide = channels // CHUNKS
    if ranks != 2 or count % 8 or taps != rows or rows % 16 or members % 4 or channels % (128 * CHUNKS):
        return general(conv_input, gate_value, out_grad, filter_taps)
    pairs = members // 2
    places = pairs // 2
    scale = 1.0 / math.sqrt(rows * ranks * members)
    (fh, fl), (bh, bl) = transforms(rows + taps)
    matrices = np.stack([
        np.concatenate([fh[:, :rows], fl[:, :rows]], 1),
        np.concatenate([fh[:, rows:], fl[:, rows:]], 1),
        np.concatenate([bh[:rows], bl[:rows]], 0),
    ])
    hbm = pl.BlockSpec(memory_space=pltpu.HBM)
    bf, f32, dma, vmem = jnp.bfloat16, jnp.float32, pltpu.SemaphoreType.DMA, pltpu.VMEM
    out, fgrad = pl.pallas_call(
        functools.partial(kernel, pairs, scale),
        out_shape=(vmem((rows, channels), bf), vmem((count, channels), f32)),
        in_specs=[hbm] * 5,
        out_specs=(pl.BlockSpec(memory_space=vmem),) * 2,
        scratch_shapes=[
            vmem((2, rows, channels), bf),
            vmem((rows, channels), bf),
            vmem((rows, channels), bf),
            vmem((rows, channels), bf),
            vmem((members, count, channels), bf),
            vmem((3, rows + taps, rows + taps), bf),
            vmem((rows + taps, channels), f32),
            vmem((rows + taps, channels), f32),
            vmem((rows + taps, channels), f32),
            vmem((places, 2, 2, count, wide), f32),
            vmem((pairs, count, channels), f32),
            vmem((pairs, count, channels), bf),
            vmem((pairs, count, channels), bf),
            vmem((places, count, channels), f32),
            vmem((places, count, channels), bf),
            vmem((places, count, channels), bf),
            vmem((places, count, channels), bf),
            vmem((places, count, channels), bf),
            vmem((ranks, count, channels), bf),
            dma((CHUNKS,)), dma, dma, dma, pltpu.SemaphoreType.REGULAR,
            dma, dma((CHUNKS,)), dma, dma((places,)), dma, dma((places,)), dma, dma,
            dma, dma((CHUNKS,)), dma, dma((CHUNKS,)), dma, dma((CHUNKS,)), dma, dma,
        ],
        compiler_params=pltpu.CompilerParams(
            collective_id=0, has_side_effects=True, vmem_limit_bytes=48_000_000
        ),
    )(*(
        pltpu.with_memory_space_constraint(x, pltpu.HBM)
        for x in (conv_input[0], gate_value[0], out_grad[0], filter_taps, jnp.asarray(matrices))
    ))
    return store(out, fgrad)


PARTS = 8


def store(grad, fgrad):
    rows, channels = grad.shape
    wide = channels // PARTS

    def body(g_ref, f_ref, g_out, f_out, sems):
        def copies():
            for k in range(PARTS):
                at = pl.ds(k * (rows // PARTS), rows // PARTS)
                yield pltpu.make_async_copy(g_ref.at[at], g_out.at[0, at], sems.at[k])
            yield pltpu.make_async_copy(f_ref, f_out, sems.at[PARTS])

        for copy in copies():
            copy.start()
        for copy in copies():
            copy.wait()

    return pl.pallas_call(
        body,
        out_shape=(
            jax.ShapeDtypeStruct((1, rows, channels), grad.dtype),
            jax.ShapeDtypeStruct(fgrad.shape, fgrad.dtype),
        ),
        in_specs=[pl.BlockSpec(memory_space=pltpu.VMEM)] * 2,
        out_specs=(pl.BlockSpec(memory_space=pl.ANY),) * 2,
        scratch_shapes=[pltpu.SemaphoreType.DMA((PARTS + 1,))],
    )(pltpu.with_memory_space_constraint(grad, pltpu.VMEM), pltpu.with_memory_space_constraint(fgrad, pltpu.VMEM))


def solution(mesh):
    in_specs = (P("dp", "ctx", None), P("dp", "ctx", None), P("dp", "ctx", None), P("dp", None))
    out_specs = (P("dp", "ctx", None), P("dp", None))
    return jax.shard_map(shards, mesh=mesh, in_specs=in_specs, out_specs=out_specs, check_vma=False)
```

```python
import functools
import math

import jax
import jax.numpy as jnp
import numpy as np
from jax import lax
from jax.experimental import pallas as pl
from jax.experimental.pallas import tpu as pltpu
from jax.sharding import PartitionSpec as P


def split(values):
    high = values.astype(jnp.bfloat16)
    return high, (values - high.astype(np.float32)).astype(jnp.bfloat16)


def transforms(length):
    half = length // 2
    angle = np.pi * np.outer(2 * np.arange(half) + 1, np.arange(length)) / length
    forward = np.concatenate([np.cos(angle), -np.sin(angle)], 0)
    inverse = np.concatenate([np.cos(angle), -np.sin(angle)], 0).T / half
    return split(forward.astype(np.float32)), split(inverse.astype(np.float32))


def dot(a, b):
    return lax.dot_general(a, b, (((1,), (0,)), ((), ())), preferred_element_type=jnp.float32)


def general(conv_input, gate_value, out_grad, filter_taps):
    inputs = conv_input[0]
    rows = inputs.shape[0]
    taps = filter_taps.shape[0] * lax.axis_size("dp")
    (fh, fl), (bh, bl) = transforms(rows + taps)
    half = (rows + taps) // 2
    mixed = (out_grad[0].astype(jnp.float32) * gate_value[0].astype(jnp.float32)).astype(
        jnp.bfloat16
    )
    devices = lax.axis_size("ctx")
    rim = lax.ppermute(mixed[:taps], "ctx", [(i + 1, i) for i in range(devices - 1)])
    full_taps = lax.all_gather(filter_taps, "dp", axis=0, tiled=True)

    def spectrum(x, first=0):
        n = x.shape[0]
        s = dot(fh[:, first : first + n], x) + dot(fl[:, first : first + n], x)
        return s[:half], s[half:]

    def back(re, im, n):
        s = jnp.concatenate([re, im], 0)
        high = s.astype(jnp.bfloat16)
        low = (s - high.astype(jnp.float32)).astype(jnp.bfloat16)
        return dot(bh[:n], high) + dot(bl[:n], high) + dot(bh[:n], low)

    xr, xi = spectrum(inputs)
    gr0, gi0 = spectrum(mixed)
    gr1, gi1 = spectrum(rim, rows)
    gr, gi = gr0 + gr1, gi0 + gi1
    partial = back(xr * gr + xi * gi, xr * gi - xi * gr, taps)
    hr, hi = spectrum(full_taps)
    grad = back(hr * gr + hi * gi, hr * gi - hi * gr, rows)
    shard_grad = lax.psum(lax.psum_scatter(partial, "dp", scatter_dimension=0, tiled=True), "ctx")
    tokens_all = rows * devices * lax.axis_size("dp")
    return (grad.astype(jnp.bfloat16)[None], shard_grad * (1.0 / math.sqrt(tokens_all)))


CHUNKS = 8
EARLY = 2
LATE = 3
MESH = pl.DeviceIdType.MESH


def kernel(
    pairs, scale,
    in_hbm, gate_hbm, cot_hbm, taps_hbm, f_hbm,
    obuf, fbuf,
    x_gc, x_in, g, inc, taps_all, f_all, xs, gs, hs, p32, own32, csrc, cbuf, half32, ysrc, ybuf,
    zsrc, zbuf, xbuf,
    ld_gc, ld_in, ld_taps, ld_f, met,
    inc_s, inc_r, tz_s, tz_r, ty_s, ty_r, tc_s, tc_r,
    c_s, c_r, y_s, y_r, z_s, z_r, x_s, x_r,
):
    dp, ctx = lax.axis_index("dp"), lax.axis_index("ctx")
    core, mine = lax.rem(dp, 2), dp // 2
    partner = dp + 1 - 2 * core
    side, place, places = lax.rem(mine, 2), mine // 2, pairs // 2
    across = 2 * (mine + 1 - 2 * side) + core
    rows, channels = g.shape
    wide = channels // CHUNKS
    middle = CHUNKS // 2
    first, last = ctx == 0, ctx == 1
    other = 1 - ctx
    f32, bf = jnp.float32, jnp.bfloat16
    count = taps_all.shape[1]
    half = rows

    def cols(c):
        return pl.ds(pl.multiple_of(c * wide, wide), wide)

    def each(n, body, start=0):
        lax.fori_loop(start, n, lambda i, z: (body(i), z)[1], 0)

    def local(src, dst, sem):
        return pltpu.make_async_copy(src, dst, sem)

    def remote(src, dst, send, recv, to):
        return pltpu.make_async_remote_copy(
            src_ref=src, dst_ref=dst, send_sem=send, recv_sem=recv, device_id=to, device_id_type=MESH
        )

    own_taps = local(taps_hbm, taps_all.at[dp], ld_taps)
    load_f = local(f_hbm, f_all, ld_f)
    load_in = local(in_hbm, x_in, ld_in)

    def loads(c):
        local(cot_hbm.at[:, cols(c)], x_gc.at[0, :, cols(c)], ld_gc.at[c]).start()
        local(gate_hbm.at[:, cols(c)], x_gc.at[1, :, cols(c)], ld_gc.at[c]).start()

    each(CHUNKS, loads)

    barrier = pltpu.get_barrier_semaphore()

    @pl.when(first)
    def _():
        pl.semaphore_signal(barrier, inc=1, device_id=(dp, other), device_id_type=MESH)

    own_taps.start()
    load_f.start()
    load_in.start()

    @pl.when(last)
    def _():
        pl.semaphore_wait(barrier, 1)
        pl.semaphore_signal(met, inc=1, device_id=(dp, other), device_id_type=MESH)

    def z_peer(k):
        return lax.rem(place + k, places)

    def z_device(k):
        return 4 * z_peer(k) + 2 * side + core

    def rim(c):
        return remote(g.at[:, cols(c)], inc.at[:, cols(c)], inc_s, inc_r.at[c], (dp, other))

    def lend(c):
        return remote(in_hbm.at[:, cols(c)], inc.at[:, cols(c)], inc_s, inc_r.at[c], (dp, other))

    def mix(c):
        both = x_gc.at[:, :, cols(c)]
        local(both, both, ld_gc.at[c]).wait()
        a = x_gc[0, :, cols(c)].astype(f32)
        b = x_gc[1, :, cols(c)].astype(f32)
        g[:, cols(c)] = (a * b).astype(bf)

        @pl.when(jnp.logical_and(last, jnp.logical_or(core == 0, c < middle)))
        def _():
            rim(c).start()

    each(CHUNKS, mix)

    @pl.when(first)
    def _():
        pl.semaphore_wait(met, 1)
        pl.semaphore_signal(barrier, inc=1, device_id=(partner, ctx), device_id_type=MESH)
        pl.semaphore_signal(barrier, inc=1, device_id=(across, ctx), device_id_type=MESH)
        for k in range(1, places):
            pl.semaphore_signal(barrier, inc=1, device_id=(z_device(k), ctx), device_id_type=MESH)
        each(CHUNKS, lambda c: lend(c).start(), middle)

    def ahead(which, x):
        return jnp.dot(f_all[which], jnp.concatenate([x, x], 0), preferred_element_type=f32)

    def correlate(a, b):
        ar, ai, br, bi = a[:half], a[half:], b[:half], b[half:]
        value = jnp.concatenate([ar * br + ai * bi, ar * bi - ai * br], 0)
        high = value.astype(bf)
        low = (value - high.astype(f32)).astype(bf)
        both = jnp.dot(f_all[2], high, preferred_element_type=f32)
        return both[:half] + both[half:] + jnp.dot(f_all[2, :half, :], low, preferred_element_type=f32)

    def chunk(i):
        return jnp.where(last, i, lax.rem(i + middle, CHUNKS))

    def emit(a, b, c):
        p32[...] = correlate(a, b).reshape(places, 2, 2, count, wide)
        for s in range(2):
            csrc[pl.ds(s * places, places), :, cols(c)] = p32[:, s, 1 - core].astype(bf)
            own32[pl.ds(s * places, places), :, cols(c)] = p32[:, s, core]

    def front(i):
        c = chunk(i)
        a, b = ahead(0, x_in[:, cols(c)]), ahead(0, g[:, cols(c)])
        gs[:, cols(c)] = b

        @pl.when(i < middle)
        def _():
            emit(a, b, c)

        @pl.when(i >= middle)
        def _():
            xs[:, cols(c)] = a

    def shard(p, s, c):
        return taps_all.at[4 * p + 2 * s + c]

    def tap_z(k):
        return remote(shard(place, side, core), shard(place, side, core), tz_s, tz_r.at[place], (z_device(k), ctx))

    def tap_y(p):
        return remote(shard(p, side, core), shard(p, side, core), ty_s, ty_r.at[p], (across, ctx))

    def tap_c(p, s):
        return remote(shard(p, s, core), shard(p, s, core), tc_s, tc_r, (partner, ctx))

    def tap_wait(p, s, sem):
        remote(shard(p, s, core), shard(p, s, core), tz_s, sem, (partner, ctx)).wait_recv()

    def pass_y(k):
        p = z_peer(k)
        tap_wait(p, side, tz_r.at[p])
        tap_y(p).start()
        tap_c(p, side).start()

    def pass_c(p):
        tap_wait(p, 1 - side, ty_r.at[p])
        tap_c(p, 1 - side).start()

    def cross(c):
        return remote(csrc.at[:, :, cols(c)], cbuf.at[:, :, cols(c)], c_s, c_r.at[c], (partner, ctx))

    def turn(c):
        return remote(ysrc.at[:, :, cols(c)], ybuf.at[:, :, cols(c)], y_s, y_r.at[c], (across, ctx))

    def spread(c, k):
        return remote(
            zsrc.at[z_peer(k), :, cols(c)], zbuf.at[place, :, cols(c)], z_s, z_r.at[c], (z_device(k), ctx)
        )

    def gathered(c):
        slots = zbuf.at[pl.ds(0, places - 1), :, cols(c)]
        return remote(slots, slots, z_s, z_r.at[c], (z_device(1), ctx))

    def swap(c):
        slot = xbuf.at[ctx, :, cols(c)]
        return remote(slot, slot, x_s, x_r, (dp, other))

    def stage2(i):
        c = chunk(i)
        cross(c).wait_recv()
        there, here = pl.ds((1 - side) * places, places), pl.ds(side * places, places)
        ysrc[:, :, cols(c)] = (own32[there, :, cols(c)] + cbuf[there, :, cols(c)].astype(f32)).astype(bf)
        turn(c).start()
        half32[:, :, cols(c)] = own32[here, :, cols(c)] + cbuf[here, :, cols(c)].astype(f32)

    def stage3(i):
        c = chunk(i)
        turn(c).wait_recv()
        total = half32[:, :, cols(c)] + ybuf[:, :, cols(c)].astype(f32)
        half32[:, :, cols(c)] = total
        zsrc[:, :, cols(c)] = total.astype(bf)
        for k in range(1, places):
            spread(c, k).start()

    def stage4(i):
        c = chunk(i)
        gathered(c).wait_recv()
        total = half32[place, :, cols(c)]
        for k in range(1, places):
            total = total + zbuf[z_peer(k), :, cols(c)].astype(f32)
        xbuf[ctx, :, cols(c)] = total.astype(bf)
        swap(c).start()

    keep, drop = other.astype(f32), ctx.astype(f32)

    def arrive(c):
        remote(inc.at[:, cols(c)], inc.at[:, cols(c)], inc_s, inc_r.at[c], (dp, other)).wait_recv()
        return ahead(1, inc[:, cols(c)])

    def meet(i):
        c = chunk(i)
        w = arrive(c)
        b = gs[:, cols(c)] + keep * w
        gs[:, cols(c)] = b
        emit(xs[:, cols(c)] - drop * w, b, c)
        cross(c).start()

    def spectrum(c):
        t = taps_all[:, :, cols(c)].astype(f32).reshape(rows, wide).astype(bf)
        hs[:, cols(c)] = ahead(0, t)

    def grad(c):
        @pl.when(jnp.logical_and(first, c >= middle))
        def _():
            gs[:, cols(c)] += arrive(c)

        obuf[:, cols(c)] = correlate(hs[:, cols(c)], gs[:, cols(c)]).astype(bf)

    def at(i, when, *actions):
        @pl.when(i == when)
        def _():
            for action in actions:
                action()

    def meet_plane():
        @pl.when(first)
        def _():
            pl.semaphore_wait(barrier, places + 1)
            pl.semaphore_signal(met, inc=1, device_id=(dp, other), device_id_type=MESH)

        @pl.when(last)
        def _():
            pl.semaphore_wait(met, 1)

        own_taps.wait()
        each(places, lambda k: tap_z(k).start(), 1)
        tap_y(place).start()
        tap_c(place, side).start()
        each(EARLY, lambda i: cross(chunk(i)).start())

    def begin(i):
        front(i)

        @pl.when(jnp.logical_and(i >= EARLY, i < middle))
        def _():
            cross(chunk(i)).start()

        at(i, EARLY - 1, meet_plane)

    load_f.wait()
    load_in.wait()
    each(CHUNKS, begin)
    each(middle, stage2)

    def follow(i):
        meet(i)
        at(i, middle, lambda: pass_y(1))
        at(i, middle + 1, lambda: each(places, pass_y, 2))
        at(i, middle + 2, lambda: each(middle, stage3))

        @pl.when(jnp.logical_and(i == middle + 1, jnp.logical_and(last, core == 1)))
        def _():
            each(CHUNKS, lambda c: rim(c).start(), middle)

        @pl.when(i < CHUNKS - 1)
        def _():
            stage2(i)

    each(CHUNKS, follow, middle)

    stage2(CHUNKS - 1)
    stage3(middle)
    stage3(middle + 1)
    each(places, pass_c)
    stage3(middle + 2)
    theirs = taps_all.at[pl.ds(0, pairs)]
    remote(theirs, theirs, tc_s, tc_r, (partner, ctx)).wait_recv()

    def spectra(c):
        spectrum(c)
        at(c, 3, lambda: stage3(CHUNKS - 1))

    each(CHUNKS, spectra)
    each(middle + 2, stage4)

    def slot(c):
        grad(c)
        at(c, 0, lambda: stage4(middle + 2))

        @pl.when(c == jnp.where(last, 1, LATE))
        def _():
            stage4(CHUNKS - 1)

    each(CHUNKS, slot)

    theirs = xbuf.at[other]
    remote(theirs, theirs, x_s, x_r, (dp, other)).wait_recv()
    fbuf[...] = (xbuf[0].astype(f32) + xbuf[1].astype(f32)) * scale

    def sent(ref, sem):
        remote(ref, ref, sem, x_r, (dp, other)).wait_send()

    sent(csrc, c_s)
    sent(ysrc, y_s)
    sent(zsrc.at[pl.ds(0, places - 1)], z_s)
    sent(xbuf.at[ctx], x_s)
    sent(taps_all.at[pl.ds(0, places - 1)], tz_s)
    sent(taps_all.at[pl.ds(0, places)], ty_s)
    sent(taps_all.at[pl.ds(0, pairs)], tc_s)

    @pl.when(last)
    def _():
        sent(g, inc_s)

    @pl.when(first)
    def _():
        sent(g.at[:, pl.ds(0, channels // 2)], inc_s)


def shards(conv_input, gate_value, out_grad, filter_taps):
    _, rows, channels = conv_input.shape
    count = filter_taps.shape[0]
    members, ranks = lax.axis_size("dp"), lax.axis_size("ctx")
    taps = count * members
    wide = channels // CHUNKS
    if ranks != 2 or count % 8 or taps != rows or rows % 16 or members % 4 or channels % (128 * CHUNKS):
        return general(conv_input, gate_value, out_grad, filter_taps)
    pairs = members // 2
    places = pairs // 2
    scale = 1.0 / math.sqrt(rows * ranks * members)
    (fh, fl), (bh, bl) = transforms(rows + taps)
    matrices = np.stack([
        np.concatenate([fh[:, :rows], fl[:, :rows]], 1),
        np.concatenate([fh[:, rows:], fl[:, rows:]], 1),
        np.concatenate([bh[:rows], bl[:rows]], 0),
    ])
    hbm = pl.BlockSpec(memory_space=pltpu.HBM)
    bf, f32, dma, vmem = jnp.bfloat16, jnp.float32, pltpu.SemaphoreType.DMA, pltpu.VMEM
    out, fgrad = pl.pallas_call(
        functools.partial(kernel, pairs, scale),
        out_shape=(vmem((rows, channels), bf), vmem((count, channels), f32)),
        in_specs=[hbm] * 5,
        out_specs=(pl.BlockSpec(memory_space=vmem),) * 2,
        scratch_shapes=[
            vmem((2, rows, channels), bf),
            vmem((rows, channels), bf),
            vmem((rows, channels), bf),
            vmem((rows, channels), bf),
            vmem((members, count, channels), bf),
            vmem((3, rows + taps, rows + taps), bf),
            vmem((rows + taps, channels), f32),
            vmem((rows + taps, channels), f32),
            vmem((rows + taps, channels), f32),
            vmem((places, 2, 2, count, wide), f32),
            vmem((pairs, count, channels), f32),
            vmem((pairs, count, channels), bf),
            vmem((pairs, count, channels), bf),
            vmem((places, count, channels), f32),
            vmem((places, count, channels), bf),
            vmem((places, count, channels), bf),
            vmem((places, count, channels), bf),
            vmem((places, count, channels), bf),
            vmem((ranks, count, channels), bf),
            dma((CHUNKS,)), dma, dma, dma, pltpu.SemaphoreType.REGULAR,
            dma, dma((CHUNKS,)), dma, dma((places,)), dma, dma((places,)), dma, dma,
            dma, dma((CHUNKS,)), dma, dma((CHUNKS,)), dma, dma((CHUNKS,)), dma, dma,
        ],
        compiler_params=pltpu.CompilerParams(
            collective_id=0, has_side_effects=True, vmem_limit_bytes=48_000_000
        ),
    )(*(
        pltpu.with_memory_space_constraint(x, pltpu.HBM)
        for x in (conv_input[0], gate_value[0], out_grad[0], filter_taps, jnp.asarray(matrices))
    ))
    return store(out, fgrad)


PARTS = 8


def store(grad, fgrad):
    rows, channels = grad.shape
    wide = channels // PARTS

    def body(g_ref, f_ref, g_out, f_out, sems):
        def copies():
            for k in range(PARTS):
                at = pl.ds(k * (rows // PARTS), rows // PARTS)
                yield pltpu.make_async_copy(g_ref.at[at], g_out.at[0, at], sems.at[k])
            yield pltpu.make_async_copy(f_ref, f_out, sems.at[PARTS])

        for copy in copies():
            copy.start()
        for copy in copies():
            copy.wait()

    return pl.pallas_call(
        body,
        out_shape=(
            jax.ShapeDtypeStruct((1, rows, channels), grad.dtype),
            jax.ShapeDtypeStruct(fgrad.shape, fgrad.dtype),
        ),
        in_specs=[pl.BlockSpec(memory_space=pltpu.VMEM)] * 2,
        out_specs=(pl.BlockSpec(memory_space=pl.ANY),) * 2,
        scratch_shapes=[pltpu.SemaphoreType.DMA((PARTS + 1,))],
    )(pltpu.with_memory_space_constraint(grad, pltpu.VMEM), pltpu.with_memory_space_constraint(fgrad, pltpu.VMEM))


def solution(mesh):
    in_specs = (P("dp", "ctx", None), P("dp", "ctx", None), P("dp", "ctx", None), P("dp", None))
    out_specs = (P("dp", "ctx", None), P("dp", None))
    return jax.shard_map(shards, mesh=mesh, in_specs=in_specs, out_specs=out_specs, check_vma=False)
```

```python
import functools
import math

import jax
import jax.numpy as jnp
import numpy as np
from jax import lax
from jax.experimental import pallas as pl
from jax.experimental.pallas import tpu as pltpu
from jax.sharding import PartitionSpec as P


def split(values):
    high = values.astype(jnp.bfloat16)
    return high, (values - high.astype(np.float32)).astype(jnp.bfloat16)


def transforms(length):
    half = length // 2
    angle = np.pi * np.outer(2 * np.arange(half) + 1, np.arange(length)) / length
    forward = np.concatenate([np.cos(angle), -np.sin(angle)], 0)
    inverse = np.concatenate([np.cos(angle), -np.sin(angle)], 0).T / half
    return split(forward.astype(np.float32)), split(inverse.astype(np.float32))


def dot(a, b):
    return lax.dot_general(a, b, (((1,), (0,)), ((), ())), preferred_element_type=jnp.float32)


def general(conv_input, gate_value, out_grad, filter_taps):
    inputs = conv_input[0]
    rows = inputs.shape[0]
    taps = filter_taps.shape[0] * lax.axis_size("dp")
    (fh, fl), (bh, bl) = transforms(rows + taps)
    half = (rows + taps) // 2
    mixed = (out_grad[0].astype(jnp.float32) * gate_value[0].astype(jnp.float32)).astype(
        jnp.bfloat16
    )
    devices = lax.axis_size("ctx")
    rim = lax.ppermute(mixed[:taps], "ctx", [(i + 1, i) for i in range(devices - 1)])
    full_taps = lax.all_gather(filter_taps, "dp", axis=0, tiled=True)

    def spectrum(x, first=0):
        n = x.shape[0]
        s = dot(fh[:, first : first + n], x) + dot(fl[:, first : first + n], x)
        return s[:half], s[half:]

    def back(re, im, n):
        s = jnp.concatenate([re, im], 0)
        high = s.astype(jnp.bfloat16)
        low = (s - high.astype(jnp.float32)).astype(jnp.bfloat16)
        return dot(bh[:n], high) + dot(bl[:n], high) + dot(bh[:n], low)

    xr, xi = spectrum(inputs)
    gr0, gi0 = spectrum(mixed)
    gr1, gi1 = spectrum(rim, rows)
    gr, gi = gr0 + gr1, gi0 + gi1
    partial = back(xr * gr + xi * gi, xr * gi - xi * gr, taps)
    hr, hi = spectrum(full_taps)
    grad = back(hr * gr + hi * gi, hr * gi - hi * gr, rows)
    shard_grad = lax.psum(lax.psum_scatter(partial, "dp", scatter_dimension=0, tiled=True), "ctx")
    tokens_all = rows * devices * lax.axis_size("dp")
    return (grad.astype(jnp.bfloat16)[None], shard_grad * (1.0 / math.sqrt(tokens_all)))


CHUNKS = 8
EARLY = 2
MESH = pl.DeviceIdType.MESH


def kernel(
    pairs, scale,
    in_hbm, gate_hbm, cot_hbm, taps_hbm, f_hbm,
    obuf, fbuf,
    x_gc, x_in, g, inc, taps_all, f_all, xs, gs, hs, p32, own32, csrc, cbuf, half32, ysrc, ybuf,
    zsrc, zbuf, xbuf, vbuf,
    ld_gc, ld_in, ld_taps, ld_f, met, line,
    inc_s, inc_r, tz_s, tz_r, ty_s, ty_r, tc_s, tc_r,
    c_s, c_r, y_s, y_r, z_s, z_r, x_s, x_r, v_s, v_r,
):
    dp, ctx = lax.axis_index("dp"), lax.axis_index("ctx")
    core, mine = lax.rem(dp, 2), dp // 2
    partner = dp + 1 - 2 * core
    side, place, places = lax.rem(mine, 2), mine // 2, pairs // 2
    across = 2 * (mine + 1 - 2 * side) + core
    rows, channels = g.shape
    wide = channels // CHUNKS
    middle = CHUNKS // 2
    first, last = ctx == 0, ctx == 1
    other = 1 - ctx
    f32, bf = jnp.float32, jnp.bfloat16
    count = taps_all.shape[1]
    half = rows

    def cols(c):
        return pl.ds(pl.multiple_of(c * wide, wide), wide)

    def each(n, body, start=0):
        lax.fori_loop(start, n, lambda i, z: (body(i), z)[1], 0)

    def local(src, dst, sem):
        return pltpu.make_async_copy(src, dst, sem)

    def remote(src, dst, send, recv, to):
        return pltpu.make_async_remote_copy(
            src_ref=src, dst_ref=dst, send_sem=send, recv_sem=recv, device_id=to, device_id_type=MESH
        )

    own_taps = local(taps_hbm, taps_all.at[dp], ld_taps)
    load_f = local(f_hbm, f_all, ld_f)
    load_in = local(in_hbm, x_in, ld_in)

    def loads(c):
        local(cot_hbm.at[:, cols(c)], x_gc.at[0, :, cols(c)], ld_gc.at[c]).start()
        local(gate_hbm.at[:, cols(c)], x_gc.at[1, :, cols(c)], ld_gc.at[c]).start()

    each(CHUNKS, loads)

    barrier = pltpu.get_barrier_semaphore()

    @pl.when(first)
    def _():
        pl.semaphore_signal(barrier, inc=1, device_id=(dp, other), device_id_type=MESH)

    own_taps.start()
    load_f.start()
    load_in.start()

    @pl.when(last)
    def _():
        pl.semaphore_wait(barrier, 1)
        pl.semaphore_signal(met, inc=1, device_id=(dp, other), device_id_type=MESH)

    def z_peer(k):
        return lax.rem(place + k, places)

    def z_device(k):
        return 4 * z_peer(k) + 2 * side + core

    def rim(c):
        return remote(g.at[:, cols(c)], inc.at[:, cols(c)], inc_s, inc_r.at[c], (dp, other))

    def lend(c):
        return remote(in_hbm.at[:, cols(c)], inc.at[:, cols(c)], inc_s, inc_r.at[c], (dp, other))

    def mix(c):
        both = x_gc.at[:, :, cols(c)]
        local(both, both, ld_gc.at[c]).wait()
        a = x_gc[0, :, cols(c)].astype(f32)
        b = x_gc[1, :, cols(c)].astype(f32)
        g[:, cols(c)] = (a * b).astype(bf)

        @pl.when(jnp.logical_and(last, jnp.logical_or(core == 0, c < middle)))
        def _():
            rim(c).start()

    each(CHUNKS, mix)

    @pl.when(first)
    def _():
        pl.semaphore_wait(met, 1)
        pl.semaphore_signal(barrier, inc=1, device_id=(partner, ctx), device_id_type=MESH)
        pl.semaphore_signal(barrier, inc=1, device_id=(across, ctx), device_id_type=MESH)
        for k in range(1, places):
            @pl.when(z_peer(k) > place)
            def _(k=k):
                pl.semaphore_signal(barrier, inc=1, device_id=(z_device(k), ctx), device_id_type=MESH)
        each(CHUNKS, lambda c: lend(c).start(), middle)

    def ahead(which, x):
        return jnp.dot(f_all[which], jnp.concatenate([x, x], 0), preferred_element_type=f32)

    def correlate(a, b):
        ar, ai, br, bi = a[:half], a[half:], b[:half], b[half:]
        value = jnp.concatenate([ar * br + ai * bi, ar * bi - ai * br], 0)
        high = value.astype(bf)
        low = (value - high.astype(f32)).astype(bf)
        both = jnp.dot(f_all[2], high, preferred_element_type=f32)
        return both[:half] + both[half:] + jnp.dot(f_all[2, :half, :], low, preferred_element_type=f32)

    def chunk(i):
        return jnp.where(last, i, lax.rem(i + middle, CHUNKS))

    def emit(a, b, c):
        p32[...] = correlate(a, b).reshape(places, 2, 2, count, wide)
        for s in range(2):
            csrc[pl.ds(s * places, places), :, cols(c)] = p32[:, s, 1 - core].astype(bf)
            own32[pl.ds(s * places, places), :, cols(c)] = p32[:, s, core]

    def front(i):
        c = chunk(i)
        a, b = ahead(0, x_in[:, cols(c)]), ahead(0, g[:, cols(c)])
        gs[:, cols(c)] = b

        @pl.when(i < middle)
        def _():
            emit(a, b, c)

        @pl.when(i >= middle)
        def _():
            xs[:, cols(c)] = a

    def shard(p, s, c):
        return taps_all.at[4 * p + 2 * s + c]

    def tap_z(k):
        return remote(shard(place, side, core), shard(place, side, core), tz_s, tz_r.at[place], (z_device(k), ctx))

    def tap_y(p):
        return remote(shard(p, side, core), shard(p, side, core), ty_s, ty_r.at[p], (across, ctx))

    def tap_c(p, s):
        return remote(shard(p, s, core), shard(p, s, core), tc_s, tc_r, (partner, ctx))

    def tap_wait(p, s, sem):
        remote(shard(p, s, core), shard(p, s, core), tz_s, sem, (partner, ctx)).wait_recv()

    def pass_y(j):
        inner = jnp.where(j == 1, places - 1, j - 1)
        p = z_peer(jnp.where(place == 0, j, jnp.where(place == places - 1, places - j, inner)))
        tap_wait(p, side, tz_r.at[p])
        tap_y(p).start()
        tap_c(p, side).start()

    def pass_c(p):
        tap_wait(p, 1 - side, ty_r.at[p])
        tap_c(p, 1 - side).start()

    def cross(c):
        return remote(csrc.at[:, :, cols(c)], cbuf.at[:, :, cols(c)], c_s, c_r.at[c], (partner, ctx))

    def turn(c):
        return remote(ysrc.at[:, :, cols(c)], ybuf.at[:, :, cols(c)], y_s, y_r.at[c], (across, ctx))

    def spread(c, k):
        return remote(
            zsrc.at[z_peer(k), :, cols(c)], zbuf.at[place, :, cols(c)], z_s, z_r.at[c], (z_device(k), ctx)
        )

    def gathered(c):
        slots = zbuf.at[pl.ds(0, places - 1), :, cols(c)]
        return remote(slots, slots, z_s, z_r.at[c], (z_device(1), ctx))

    def swap(c):
        slot = xbuf.at[ctx, :, cols(c)]
        return remote(slot, slot, x_s, x_r, (dp, other))

    def stage2(i):
        c = chunk(i)
        cross(c).wait_recv()
        there, here = pl.ds((1 - side) * places, places), pl.ds(side * places, places)
        ysrc[:, :, cols(c)] = (own32[there, :, cols(c)] + cbuf[there, :, cols(c)].astype(f32)).astype(bf)
        turn(c).start()
        half32[:, :, cols(c)] = own32[here, :, cols(c)] + cbuf[here, :, cols(c)].astype(f32)

    def stage3(i):
        c = chunk(i)
        turn(c).wait_recv()
        total = half32[:, :, cols(c)] + ybuf[:, :, cols(c)].astype(f32)
        half32[:, :, cols(c)] = total
        zsrc[:, :, cols(c)] = total.astype(bf)
        for k in range(1, places):
            spread(c, k).start()

    def stage4(i):
        c = chunk(i)
        gathered(c).wait_recv()
        total = half32[place, :, cols(c)]
        for k in range(1, places):
            total = total + zbuf[z_peer(k), :, cols(c)].astype(f32)
        xbuf[ctx, :, cols(c)] = total.astype(bf)
        swap(c).start()

    tail = chunk(CHUNKS - 1)
    theirs_tail = jnp.where(last, middle - 1, CHUNKS - 1)
    few = pl.ds(0, channels - wide)

    def direct(k, to):
        return remote(
            zsrc.at[z_peer(k), :, cols(tail)], vbuf.at[ctx * places + place], v_s, v_r, (z_device(k), to)
        )

    def finish3():
        turn(tail).wait_recv()
        total = half32[:, :, cols(tail)] + ybuf[:, :, cols(tail)].astype(f32)
        zsrc[:, :, cols(tail)] = total.astype(bf)
        for k in range(1, places):
            direct(k, other).start()
        direct(0, other).start()
        for k in range(1, places):
            direct(k, ctx).start()
        vbuf[ctx * places + place] = zsrc[place, :, cols(tail)]

    def summed(r):
        total = vbuf[r * places].astype(f32)
        for p in range(1, places):
            total = total + vbuf[r * places + p].astype(f32)
        return total.astype(bf)

    keep, drop = other.astype(f32), ctx.astype(f32)

    def arrive(c):
        remote(inc.at[:, cols(c)], inc.at[:, cols(c)], inc_s, inc_r.at[c], (dp, other)).wait_recv()
        return ahead(1, inc[:, cols(c)])

    def meet(i):
        c = chunk(i)
        w = arrive(c)
        b = gs[:, cols(c)] + keep * w
        gs[:, cols(c)] = b
        emit(xs[:, cols(c)] - drop * w, b, c)
        cross(c).start()

    def spectrum(c):
        t = taps_all[:, :, cols(c)].astype(f32).reshape(rows, wide).astype(bf)
        hs[:, cols(c)] = ahead(0, t)

    def grad(c):
        @pl.when(jnp.logical_and(first, c >= middle))
        def _():
            gs[:, cols(c)] += arrive(c)

        obuf[:, cols(c)] = correlate(hs[:, cols(c)], gs[:, cols(c)]).astype(bf)

    def at(i, when, *actions):
        @pl.when(i == when)
        def _():
            for action in actions:
                action()

    def meet_plane():
        @pl.when(first)
        def _():
            pl.semaphore_wait(barrier, 2 + place)
            pl.semaphore_signal(met, inc=1, device_id=(dp, other), device_id_type=MESH)
            for k in range(1, places):
                @pl.when(z_peer(k) < place)
                def _(k=k):
                    pl.semaphore_signal(line, inc=1, device_id=(z_device(k), ctx), device_id_type=MESH)

        @pl.when(last)
        def _():
            pl.semaphore_wait(met, 1)

        own_taps.wait()

        def lower(k):
            @pl.when(z_peer(k) < place)
            def _():
                tap_z(k).start()

        each(places, lower, 1)
        tap_y(place).start()
        tap_c(place, side).start()
        each(EARLY, lambda i: cross(chunk(i)).start())

    def meet_line():
        @pl.when(first)
        def _():
            @pl.when(place < places - 1)
            def _():
                pl.semaphore_wait(line, places - 1 - place)

            pl.semaphore_signal(line, inc=1, device_id=(dp, other), device_id_type=MESH)

        @pl.when(last)
        def _():
            pl.semaphore_wait(line, 1)

        def upper(k):
            @pl.when(z_peer(k) > place)
            def _():
                tap_z(k).start()

        each(places, upper, 1)

    def begin(i):
        front(i)

        @pl.when(jnp.logical_and(i >= EARLY, i < middle))
        def _():
            cross(chunk(i)).start()

        at(i, EARLY - 1, meet_plane)

        @pl.when(i == jnp.where(place == places - 1, EARLY - 1, jnp.where(place == 0, CHUNKS - 1, CHUNKS - 3)))
        def _():
            meet_line()

        at(i, CHUNKS - 3, lambda: each(middle, stage2))

    load_f.wait()
    load_in.wait()
    each(CHUNKS, begin)

    def follow(i):
        meet(i)
        at(i, middle, lambda: pass_y(1))
        at(i, middle + 1, lambda: each(places, pass_y, 2))
        at(i, middle + 2, lambda: each(middle, stage3))

        @pl.when(jnp.logical_and(i == CHUNKS - 1, jnp.logical_and(last, core == 1)))
        def _():
            each(CHUNKS, lambda c: rim(c).start(), middle)

        @pl.when(i < CHUNKS - 1)
        def _():
            stage2(i)

    each(CHUNKS, follow, middle)

    stage2(CHUNKS - 1)
    stage3(middle)
    stage3(middle + 1)
    each(places, pass_c)
    stage3(middle + 2)
    theirs = taps_all.at[pl.ds(0, pairs)]
    remote(theirs, theirs, tc_s, tc_r, (partner, ctx)).wait_recv()

    def spectra(c):
        spectrum(c)
        at(c, 3, finish3)

    each(CHUNKS, spectra)

    def slot(c):
        grad(c)
        at(c, middle - 1, lambda: each(CHUNKS - 1, stage4))

    each(CHUNKS, slot)

    theirs = xbuf.at[other, :, few]
    remote(theirs, theirs, x_s, x_r, (dp, other)).wait_recv()
    theirs = vbuf.at[pl.ds(0, 2 * places - 1)]
    remote(theirs, theirs, v_s, v_r, (dp, other)).wait_recv()
    mine_x = xbuf.at[ctx, :, few]
    remote(mine_x, mine_x, x_s, x_r, (dp, other)).wait_send()
    xbuf[ctx, :, cols(tail)] = summed(ctx)
    xbuf[other, :, cols(theirs_tail)] = summed(other)
    fbuf[...] = (xbuf[0].astype(f32) + xbuf[1].astype(f32)) * scale

    def sent(ref, sem):
        remote(ref, ref, sem, x_r, (dp, other)).wait_send()

    sent(csrc, c_s)
    sent(ysrc, y_s)
    sent(zsrc.at[pl.ds(0, places - 1), :, few], z_s)
    sent(vbuf.at[pl.ds(0, 2 * places - 1)], v_s)
    sent(taps_all.at[pl.ds(0, places - 1)], tz_s)
    sent(taps_all.at[pl.ds(0, places)], ty_s)
    sent(taps_all.at[pl.ds(0, pairs)], tc_s)

    @pl.when(last)
    def _():
        sent(g, inc_s)

    @pl.when(first)
    def _():
        sent(g.at[:, pl.ds(0, channels // 2)], inc_s)


def shards(conv_input, gate_value, out_grad, filter_taps):
    _, rows, channels = conv_input.shape
    count = filter_taps.shape[0]
    members, ranks = lax.axis_size("dp"), lax.axis_size("ctx")
    taps = count * members
    wide = channels // CHUNKS
    if ranks != 2 or count % 8 or taps != rows or rows % 16 or members % 4 or channels % (128 * CHUNKS):
        return general(conv_input, gate_value, out_grad, filter_taps)
    pairs = members // 2
    places = pairs // 2
    scale = 1.0 / math.sqrt(rows * ranks * members)
    (fh, fl), (bh, bl) = transforms(rows + taps)
    matrices = np.stack([
        np.concatenate([fh[:, :rows], fl[:, :rows]], 1),
        np.concatenate([fh[:, rows:], fl[:, rows:]], 1),
        np.concatenate([bh[:rows], bl[:rows]], 0),
    ])
    hbm = pl.BlockSpec(memory_space=pltpu.HBM)
    bf, f32, dma, vmem = jnp.bfloat16, jnp.float32, pltpu.SemaphoreType.DMA, pltpu.VMEM
    out, fgrad = pl.pallas_call(
        functools.partial(kernel, pairs, scale),
        out_shape=(vmem((rows, channels), bf), vmem((count, channels), f32)),
        in_specs=[hbm] * 5,
        out_specs=(pl.BlockSpec(memory_space=vmem),) * 2,
        scratch_shapes=[
            vmem((2, rows, channels), bf),
            vmem((rows, channels), bf),
            vmem((rows, channels), bf),
            vmem((rows, channels), bf),
            vmem((members, count, channels), bf),
            vmem((3, rows + taps, rows + taps), bf),
            vmem((rows + taps, channels), f32),
            vmem((rows + taps, channels), f32),
            vmem((rows + taps, channels), f32),
            vmem((places, 2, 2, count, wide), f32),
            vmem((pairs, count, channels), f32),
            vmem((pairs, count, channels), bf),
            vmem((pairs, count, channels), bf),
            vmem((places, count, channels), f32),
            vmem((places, count, channels), bf),
            vmem((places, count, channels), bf),
            vmem((places, count, channels), bf),
            vmem((places, count, channels), bf),
            vmem((ranks, count, channels), bf),
            vmem((2 * places, count, wide), bf),
            dma((CHUNKS,)), dma, dma, dma, pltpu.SemaphoreType.REGULAR, pltpu.SemaphoreType.REGULAR,
            dma, dma((CHUNKS,)), dma, dma((places,)), dma, dma((places,)), dma, dma,
            dma, dma((CHUNKS,)), dma, dma((CHUNKS,)), dma, dma((CHUNKS,)), dma, dma, dma, dma,
        ],
        compiler_params=pltpu.CompilerParams(
            collective_id=0, has_side_effects=True, vmem_limit_bytes=48_000_000
        ),
    )(*(
        pltpu.with_memory_space_constraint(x, pltpu.HBM)
        for x in (conv_input[0], gate_value[0], out_grad[0], filter_taps, jnp.asarray(matrices))
    ))
    return store(out, fgrad)


PARTS = 8


def store(grad, fgrad):
    rows, channels = grad.shape
    wide = channels // PARTS

    def body(g_ref, f_ref, g_out, f_out, sems):
        def copies():
            for k in range(PARTS):
                at = pl.ds(k * (rows // PARTS), rows // PARTS)
                yield pltpu.make_async_copy(g_ref.at[at], g_out.at[0, at], sems.at[k])
            yield pltpu.make_async_copy(f_ref, f_out, sems.at[PARTS])

        for copy in copies():
            copy.start()
        for copy in copies():
            copy.wait()

    return pl.pallas_call(
        body,
        out_shape=(
            jax.ShapeDtypeStruct((1, rows, channels), grad.dtype),
            jax.ShapeDtypeStruct(fgrad.shape, fgrad.dtype),
        ),
        in_specs=[pl.BlockSpec(memory_space=pltpu.VMEM)] * 2,
        out_specs=(pl.BlockSpec(memory_space=pl.ANY),) * 2,
        scratch_shapes=[pltpu.SemaphoreType.DMA((PARTS + 1,))],
    )(pltpu.with_memory_space_constraint(grad, pltpu.VMEM), pltpu.with_memory_space_constraint(fgrad, pltpu.VMEM))


def solution(mesh):
    in_specs = (P("dp", "ctx", None), P("dp", "ctx", None), P("dp", "ctx", None), P("dp", None))
    out_specs = (P("dp", "ctx", None), P("dp", None))
    return jax.shard_map(shards, mesh=mesh, in_specs=in_specs, out_specs=out_specs, check_vma=False)
```

```python
import functools
import math

import jax
import jax.numpy as jnp
import numpy as np
from jax import lax
from jax.experimental import pallas as pl
from jax.experimental.pallas import tpu as pltpu
from jax.sharding import PartitionSpec as P


def split(values):
    high = values.astype(jnp.bfloat16)
    return high, (values - high.astype(np.float32)).astype(jnp.bfloat16)


def transforms(length):
    half = length // 2
    angle = np.pi * np.outer(2 * np.arange(half) + 1, np.arange(length)) / length
    forward = np.concatenate([np.cos(angle), -np.sin(angle)], 0)
    inverse = np.concatenate([np.cos(angle), -np.sin(angle)], 0).T / half
    return split(forward.astype(np.float32)), split(inverse.astype(np.float32))


def dot(a, b):
    return lax.dot_general(a, b, (((1,), (0,)), ((), ())), preferred_element_type=jnp.float32)


def general(conv_input, gate_value, out_grad, filter_taps):
    inputs = conv_input[0]
    rows = inputs.shape[0]
    taps = filter_taps.shape[0] * lax.axis_size("dp")
    (fh, fl), (bh, bl) = transforms(rows + taps)
    half = (rows + taps) // 2
    mixed = (out_grad[0].astype(jnp.float32) * gate_value[0].astype(jnp.float32)).astype(
        jnp.bfloat16
    )
    devices = lax.axis_size("ctx")
    rim = lax.ppermute(mixed[:taps], "ctx", [(i + 1, i) for i in range(devices - 1)])
    full_taps = lax.all_gather(filter_taps, "dp", axis=0, tiled=True)

    def spectrum(x, first=0):
        n = x.shape[0]
        s = dot(fh[:, first : first + n], x) + dot(fl[:, first : first + n], x)
        return s[:half], s[half:]

    def back(re, im, n):
        s = jnp.concatenate([re, im], 0)
        high = s.astype(jnp.bfloat16)
        low = (s - high.astype(jnp.float32)).astype(jnp.bfloat16)
        return dot(bh[:n], high) + dot(bl[:n], high) + dot(bh[:n], low)

    xr, xi = spectrum(inputs)
    gr0, gi0 = spectrum(mixed)
    gr1, gi1 = spectrum(rim, rows)
    gr, gi = gr0 + gr1, gi0 + gi1
    partial = back(xr * gr + xi * gi, xr * gi - xi * gr, taps)
    hr, hi = spectrum(full_taps)
    grad = back(hr * gr + hi * gi, hr * gi - hi * gr, rows)
    shard_grad = lax.psum(lax.psum_scatter(partial, "dp", scatter_dimension=0, tiled=True), "ctx")
    tokens_all = rows * devices * lax.axis_size("dp")
    return (grad.astype(jnp.bfloat16)[None], shard_grad * (1.0 / math.sqrt(tokens_all)))


CHUNKS = 8
EARLY = 2
FIRST = 4
MESH = pl.DeviceIdType.MESH


def kernel(
    pairs, scale,
    in_hbm, gate_hbm, cot_hbm, taps_hbm, f_hbm,
    obuf, fbuf,
    x_gc, x_in, g, inc, taps_all, f_all, xs, gs, hs, p32, own32, csrc, cbuf, half32, ysrc, ybuf,
    zsrc, zbuf, xbuf, vbuf,
    ld_gc, ld_in, ld_taps, ld_f, met, line,
    inc_s, inc_r, tz_s, tz_r, ty_s, ty_r, tc_s, tc_r,
    c_s, c_r, y_s, y_r, z_s, z_r, x_s, x_r, v_s, v_r,
):
    dp, ctx = lax.axis_index("dp"), lax.axis_index("ctx")
    core, mine = lax.rem(dp, 2), dp // 2
    partner = dp + 1 - 2 * core
    side, place, places = lax.rem(mine, 2), mine // 2, pairs // 2
    across = 2 * (mine + 1 - 2 * side) + core
    rows, channels = g.shape
    wide = channels // CHUNKS
    middle = CHUNKS // 2
    first, last = ctx == 0, ctx == 1
    other = 1 - ctx
    f32, bf = jnp.float32, jnp.bfloat16
    count = taps_all.shape[1]
    half = rows

    def cols(c):
        return pl.ds(pl.multiple_of(c * wide, wide), wide)

    def each(n, body, start=0):
        lax.fori_loop(start, n, lambda i, z: (body(i), z)[1], 0)

    def local(src, dst, sem):
        return pltpu.make_async_copy(src, dst, sem)

    def remote(src, dst, send, recv, to):
        return pltpu.make_async_remote_copy(
            src_ref=src, dst_ref=dst, send_sem=send, recv_sem=recv, device_id=to, device_id_type=MESH
        )

    own_taps = local(taps_hbm, taps_all.at[dp], ld_taps)
    load_f = local(f_hbm, f_all, ld_f)
    load_in = local(in_hbm, x_in, ld_in)

    def loads(c):
        local(cot_hbm.at[:, cols(c)], x_gc.at[0, :, cols(c)], ld_gc.at[lax.min(c, 1)]).start()
        local(gate_hbm.at[:, cols(c)], x_gc.at[1, :, cols(c)], ld_gc.at[lax.min(c, 1)]).start()

    each(CHUNKS, loads)

    barrier = pltpu.get_barrier_semaphore()

    @pl.when(first)
    def _():
        pl.semaphore_signal(barrier, inc=1, device_id=(dp, other), device_id_type=MESH)

    own_taps.start()
    load_f.start()
    load_in.start()

    @pl.when(last)
    def _():
        pl.semaphore_wait(barrier, 1)
        pl.semaphore_signal(met, inc=1, device_id=(dp, other), device_id_type=MESH)

    def z_peer(k):
        return lax.rem(place + k, places)

    def z_device(k):
        return 4 * z_peer(k) + 2 * side + core

    def rim(c):
        return remote(g.at[:, cols(c)], inc.at[:, cols(c)], inc_s, inc_r.at[c], (dp, other))

    def lend(c):
        return remote(in_hbm.at[:, cols(c)], inc.at[:, cols(c)], inc_s, inc_r.at[c], (dp, other))

    def mix(c):
        a = x_gc[0, :, cols(c)].astype(f32)
        b = x_gc[1, :, cols(c)].astype(f32)
        g[:, cols(c)] = (a * b).astype(bf)

        @pl.when(jnp.logical_and(last, jnp.logical_or(core == 0, c < FIRST)))
        def _():
            rim(c).start()

    def loaded(at, k):
        both = x_gc.at[:, :, at]
        local(both, both, ld_gc.at[k]).wait()

    loaded(pl.ds(0, wide), 0)
    mix(jnp.int32(0))
    loaded(pl.ds(wide, channels - wide), 1)
    each(CHUNKS, mix, 1)

    @pl.when(first)
    def _():
        pl.semaphore_wait(met, 1)
        pl.semaphore_signal(barrier, inc=1, device_id=(partner, ctx), device_id_type=MESH)
        pl.semaphore_signal(barrier, inc=1, device_id=(across, ctx), device_id_type=MESH)
        for k in range(1, places):
            @pl.when(z_peer(k) > place)
            def _(k=k):
                pl.semaphore_signal(barrier, inc=1, device_id=(z_device(k), ctx), device_id_type=MESH)
        each(CHUNKS, lambda c: lend(c).start(), middle)

    def ahead(which, x):
        return jnp.dot(f_all[which], jnp.concatenate([x, x], 0), preferred_element_type=f32)

    def correlate(a, b):
        ar, ai, br, bi = a[:half], a[half:], b[:half], b[half:]
        value = jnp.concatenate([ar * br + ai * bi, ar * bi - ai * br], 0)
        high = value.astype(bf)
        low = (value - high.astype(f32)).astype(bf)
        both = jnp.dot(f_all[2], high, preferred_element_type=f32)
        return both[:half] + both[half:] + jnp.dot(f_all[2, :half, :], low, preferred_element_type=f32)

    def chunk(i):
        return jnp.where(last, i, lax.rem(i + middle, CHUNKS))

    def emit(a, b, c):
        p32[...] = correlate(a, b).reshape(places, 2, 2, count, wide)
        for s in range(2):
            csrc[pl.ds(s * places, places), :, cols(c)] = p32[:, s, 1 - core].astype(bf)
            own32[pl.ds(s * places, places), :, cols(c)] = p32[:, s, core]

    def front(i):
        c = chunk(i)
        a, b = ahead(0, x_in[:, cols(c)]), ahead(0, g[:, cols(c)])
        gs[:, cols(c)] = b

        @pl.when(i < middle)
        def _():
            emit(a, b, c)

        @pl.when(i >= middle)
        def _():
            xs[:, cols(c)] = a

    def shard(p, s, c):
        return taps_all.at[4 * p + 2 * s + c]

    def tap_z(k):
        return remote(shard(place, side, core), shard(place, side, core), tz_s, tz_r.at[place], (z_device(k), ctx))

    def tap_y(p):
        return remote(shard(p, side, core), shard(p, side, core), ty_s, ty_r.at[p], (across, ctx))

    def tap_c(p, s):
        return remote(shard(p, s, core), shard(p, s, core), tc_s, tc_r, (partner, ctx))

    def tap_wait(p, s, sem):
        remote(shard(p, s, core), shard(p, s, core), tz_s, sem, (partner, ctx)).wait_recv()

    def pass_y(j):
        inner = jnp.where(j == 1, places - 1, j - 1)
        p = z_peer(jnp.where(place == 0, j, jnp.where(place == places - 1, places - j, inner)))
        tap_wait(p, side, tz_r.at[p])
        tap_y(p).start()
        tap_c(p, side).start()

    def pass_c(p):
        tap_wait(p, 1 - side, ty_r.at[p])
        tap_c(p, 1 - side).start()

    def cross(c):
        return remote(csrc.at[:, :, cols(c)], cbuf.at[:, :, cols(c)], c_s, c_r.at[c], (partner, ctx))

    def turn(c):
        return remote(ysrc.at[:, :, cols(c)], ybuf.at[:, :, cols(c)], y_s, y_r.at[c], (across, ctx))

    def spread(c, k):
        return remote(
            zsrc.at[z_peer(k), :, cols(c)], zbuf.at[place, :, cols(c)], z_s, z_r.at[c], (z_device(k), ctx)
        )

    def gathered(c):
        slots = zbuf.at[pl.ds(0, places - 1), :, cols(c)]
        return remote(slots, slots, z_s, z_r.at[c], (z_device(1), ctx))

    def swap(c):
        slot = xbuf.at[ctx, :, cols(c)]
        return remote(slot, slot, x_s, x_r, (dp, other))

    def stage2(i):
        c = chunk(i)
        cross(c).wait_recv()
        there, here = pl.ds((1 - side) * places, places), pl.ds(side * places, places)
        ysrc[:, :, cols(c)] = (own32[there, :, cols(c)] + cbuf[there, :, cols(c)].astype(f32)).astype(bf)
        turn(c).start()
        half32[:, :, cols(c)] = own32[here, :, cols(c)] + cbuf[here, :, cols(c)].astype(f32)

    def stage3(i):
        c = chunk(i)
        turn(c).wait_recv()
        total = half32[:, :, cols(c)] + ybuf[:, :, cols(c)].astype(f32)
        half32[:, :, cols(c)] = total
        zsrc[:, :, cols(c)] = total.astype(bf)
        for k in range(1, places):
            spread(c, k).start()

    def stage4(i):
        c = chunk(i)
        gathered(c).wait_recv()
        total = half32[place, :, cols(c)]
        for k in range(1, places):
            total = total + zbuf[z_peer(k), :, cols(c)].astype(f32)
        xbuf[ctx, :, cols(c)] = total.astype(bf)
        swap(c).start()

    tail = chunk(CHUNKS - 1)
    theirs_tail = jnp.where(last, middle - 1, CHUNKS - 1)
    few = pl.ds(0, channels - wide)

    def direct(k, to):
        return remote(
            zsrc.at[z_peer(k), :, cols(tail)], vbuf.at[ctx * places + place], v_s, v_r, (z_device(k), to)
        )

    def finish3():
        turn(tail).wait_recv()
        total = half32[:, :, cols(tail)] + ybuf[:, :, cols(tail)].astype(f32)
        zsrc[:, :, cols(tail)] = total.astype(bf)
        for k in range(1, places):
            direct(k, other).start()
        direct(0, other).start()
        for k in range(1, places):
            direct(k, ctx).start()
        vbuf[ctx * places + place] = zsrc[place, :, cols(tail)]

    def summed(r):
        total = vbuf[r * places].astype(f32)
        for p in range(1, places):
            total = total + vbuf[r * places + p].astype(f32)
        return total.astype(bf)

    keep, drop = other.astype(f32), ctx.astype(f32)

    def arrive(c):
        remote(inc.at[:, cols(c)], inc.at[:, cols(c)], inc_s, inc_r.at[c], (dp, other)).wait_recv()
        return ahead(1, inc[:, cols(c)])

    def meet(i):
        c = chunk(i)
        w = arrive(c)
        b = gs[:, cols(c)] + keep * w
        gs[:, cols(c)] = b
        emit(xs[:, cols(c)] - drop * w, b, c)
        cross(c).start()

    def spectrum(c):
        t = taps_all[:, :, cols(c)].astype(f32).reshape(rows, wide).astype(bf)
        hs[:, cols(c)] = ahead(0, t)

    def grad(c):
        @pl.when(jnp.logical_and(first, c >= middle))
        def _():
            gs[:, cols(c)] += arrive(c)

        obuf[:, cols(c)] = correlate(hs[:, cols(c)], gs[:, cols(c)]).astype(bf)

    def at(i, when, *actions):
        @pl.when(i == when)
        def _():
            for action in actions:
                action()

    def meet_plane():
        @pl.when(first)
        def _():
            pl.semaphore_wait(barrier, 2 + place)
            pl.semaphore_signal(met, inc=1, device_id=(dp, other), device_id_type=MESH)
            for k in range(1, places):
                @pl.when(z_peer(k) < place)
                def _(k=k):
                    pl.semaphore_signal(line, inc=1, device_id=(z_device(k), ctx), device_id_type=MESH)

        @pl.when(last)
        def _():
            pl.semaphore_wait(met, 1)

        own_taps.wait()

        def lower(k):
            @pl.when(z_peer(k) < place)
            def _():
                tap_z(k).start()

        each(places, lower, 1)
        tap_y(place).start()
        tap_c(place, side).start()
        each(EARLY, lambda i: cross(chunk(i)).start())

    def meet_line():
        @pl.when(first)
        def _():
            @pl.when(place < places - 1)
            def _():
                pl.semaphore_wait(line, places - 1 - place)

            pl.semaphore_signal(line, inc=1, device_id=(dp, other), device_id_type=MESH)

        @pl.when(last)
        def _():
            pl.semaphore_wait(line, 1)

        def upper(k):
            @pl.when(z_peer(k) > place)
            def _():
                tap_z(k).start()

        each(places, upper, 1)

    def begin(i):
        front(i)

        @pl.when(jnp.logical_and(i >= EARLY, i < middle))
        def _():
            cross(chunk(i)).start()

        at(i, EARLY - 1, meet_plane)

        @pl.when(i == jnp.where(place == places - 1, EARLY - 1, jnp.where(place == 0, CHUNKS - 1, CHUNKS - 3)))
        def _():
            meet_line()

        at(i, CHUNKS - 3, lambda: each(middle, stage2))

    load_f.wait()
    load_in.wait()
    each(CHUNKS, begin)

    def follow(i):
        meet(i)
        at(i, middle, lambda: pass_y(1))
        at(i, middle + 1, lambda: each(places, pass_y, 2))
        at(i, middle + 2, lambda: each(middle, stage3))

        @pl.when(jnp.logical_and(i == CHUNKS - 1, jnp.logical_and(last, core == 1)))
        def _():
            each(CHUNKS, lambda c: rim(c).start(), FIRST)

        @pl.when(i < CHUNKS - 1)
        def _():
            stage2(i)

    each(CHUNKS, follow, middle)

    stage2(CHUNKS - 1)
    stage3(middle)
    stage3(middle + 1)
    each(places, pass_c)
    stage3(middle + 2)
    theirs = taps_all.at[pl.ds(0, pairs)]
    remote(theirs, theirs, tc_s, tc_r, (partner, ctx)).wait_recv()

    def spectra(c):
        spectrum(c)
        at(c, 3, finish3)

    each(CHUNKS, spectra)

    def slot(c):
        grad(c)
        at(c, middle - 1, lambda: each(CHUNKS - 1, stage4))

    each(CHUNKS, slot)

    theirs = xbuf.at[other, :, few]
    remote(theirs, theirs, x_s, x_r, (dp, other)).wait_recv()
    theirs = vbuf.at[pl.ds(0, 2 * places - 1)]
    remote(theirs, theirs, v_s, v_r, (dp, other)).wait_recv()
    mine_x = xbuf.at[ctx, :, few]
    remote(mine_x, mine_x, x_s, x_r, (dp, other)).wait_send()
    xbuf[ctx, :, cols(tail)] = summed(ctx)
    xbuf[other, :, cols(theirs_tail)] = summed(other)
    fbuf[...] = (xbuf[0].astype(f32) + xbuf[1].astype(f32)) * scale

    def sent(ref, sem):
        remote(ref, ref, sem, x_r, (dp, other)).wait_send()

    sent(csrc, c_s)
    sent(ysrc, y_s)
    sent(zsrc.at[pl.ds(0, places - 1), :, few], z_s)
    sent(vbuf.at[pl.ds(0, 2 * places - 1)], v_s)
    sent(taps_all.at[pl.ds(0, places - 1)], tz_s)
    sent(taps_all.at[pl.ds(0, places)], ty_s)
    sent(taps_all.at[pl.ds(0, pairs)], tc_s)

    @pl.when(last)
    def _():
        sent(g, inc_s)

    @pl.when(first)
    def _():
        sent(g.at[:, pl.ds(0, channels // 2)], inc_s)


def shards(conv_input, gate_value, out_grad, filter_taps):
    _, rows, channels = conv_input.shape
    count = filter_taps.shape[0]
    members, ranks = lax.axis_size("dp"), lax.axis_size("ctx")
    taps = count * members
    wide = channels // CHUNKS
    if ranks != 2 or count % 8 or taps != rows or rows % 16 or members % 4 or channels % (128 * CHUNKS):
        return general(conv_input, gate_value, out_grad, filter_taps)
    pairs = members // 2
    places = pairs // 2
    scale = 1.0 / math.sqrt(rows * ranks * members)
    (fh, fl), (bh, bl) = transforms(rows + taps)
    matrices = np.stack([
        np.concatenate([fh[:, :rows], fl[:, :rows]], 1),
        np.concatenate([fh[:, rows:], fl[:, rows:]], 1),
        np.concatenate([bh[:rows], bl[:rows]], 0),
    ])
    hbm = pl.BlockSpec(memory_space=pltpu.HBM)
    bf, f32, dma, vmem = jnp.bfloat16, jnp.float32, pltpu.SemaphoreType.DMA, pltpu.VMEM
    out, fgrad = pl.pallas_call(
        functools.partial(kernel, pairs, scale),
        out_shape=(vmem((rows, channels), bf), vmem((count, channels), f32)),
        in_specs=[hbm] * 5,
        out_specs=(pl.BlockSpec(memory_space=vmem),) * 2,
        scratch_shapes=[
            vmem((2, rows, channels), bf),
            vmem((rows, channels), bf),
            vmem((rows, channels), bf),
            vmem((rows, channels), bf),
            vmem((members, count, channels), bf),
            vmem((3, rows + taps, rows + taps), bf),
            vmem((rows + taps, channels), f32),
            vmem((rows + taps, channels), f32),
            vmem((rows + taps, channels), f32),
            vmem((places, 2, 2, count, wide), f32),
            vmem((pairs, count, channels), f32),
            vmem((pairs, count, channels), bf),
            vmem((pairs, count, channels), bf),
            vmem((places, count, channels), f32),
            vmem((places, count, channels), bf),
            vmem((places, count, channels), bf),
            vmem((places, count, channels), bf),
            vmem((places, count, channels), bf),
            vmem((ranks, count, channels), bf),
            vmem((2 * places, count, wide), bf),
            dma((2,)), dma, dma, dma, pltpu.SemaphoreType.REGULAR, pltpu.SemaphoreType.REGULAR,
            dma, dma((CHUNKS,)), dma, dma((places,)), dma, dma((places,)), dma, dma,
            dma, dma((CHUNKS,)), dma, dma((CHUNKS,)), dma, dma((CHUNKS,)), dma, dma, dma, dma,
        ],
        compiler_params=pltpu.CompilerParams(
            collective_id=0, has_side_effects=True, vmem_limit_bytes=48_000_000
        ),
    )(*(
        pltpu.with_memory_space_constraint(x, pltpu.HBM)
        for x in (conv_input[0], gate_value[0], out_grad[0], filter_taps, jnp.asarray(matrices))
    ))
    return store(out, fgrad)


PARTS = 1


def store(grad, fgrad):
    rows, channels = grad.shape
    wide = channels // PARTS

    def body(g_ref, f_ref, g_out, f_out, sems):
        def copies():
            for k in range(PARTS):
                at = pl.ds(k * (rows // PARTS), rows // PARTS)
                yield pltpu.make_async_copy(g_ref.at[at], g_out.at[0, at], sems.at[k])
            yield pltpu.make_async_copy(f_ref, f_out, sems.at[PARTS])

        for copy in copies():
            copy.start()
        for copy in copies():
            copy.wait()

    return pl.pallas_call(
        body,
        out_shape=(
            jax.ShapeDtypeStruct((1, rows, channels), grad.dtype),
            jax.ShapeDtypeStruct(fgrad.shape, fgrad.dtype),
        ),
        in_specs=[pl.BlockSpec(memory_space=pltpu.VMEM)] * 2,
        out_specs=(pl.BlockSpec(memory_space=pl.ANY),) * 2,
        scratch_shapes=[pltpu.SemaphoreType.DMA((PARTS + 1,))],
    )(pltpu.with_memory_space_constraint(grad, pltpu.VMEM), pltpu.with_memory_space_constraint(fgrad, pltpu.VMEM))


def solution(mesh):
    in_specs = (P("dp", "ctx", None), P("dp", "ctx", None), P("dp", "ctx", None), P("dp", None))
    out_specs = (P("dp", "ctx", None), P("dp", None))
    return jax.shard_map(shards, mesh=mesh, in_specs=in_specs, out_specs=out_specs, check_vma=False)
```

```python
import functools
import math

import jax
import jax.numpy as jnp
import numpy as np
from jax import lax
from jax.experimental import pallas as pl
from jax.experimental.pallas import tpu as pltpu
from jax.sharding import PartitionSpec as P


def split(values):
    high = values.astype(jnp.bfloat16)
    return high, (values - high.astype(np.float32)).astype(jnp.bfloat16)


def transforms(length):
    half = length // 2
    angle = np.pi * np.outer(2 * np.arange(half) + 1, np.arange(length)) / length
    forward = np.concatenate([np.cos(angle), -np.sin(angle)], 0)
    inverse = np.concatenate([np.cos(angle), -np.sin(angle)], 0).T / half
    return split(forward.astype(np.float32)), split(inverse.astype(np.float32))


def dot(a, b):
    return lax.dot_general(a, b, (((1,), (0,)), ((), ())), preferred_element_type=jnp.float32)


def general(conv_input, gate_value, out_grad, filter_taps):
    inputs = conv_input[0]
    rows = inputs.shape[0]
    taps = filter_taps.shape[0] * lax.axis_size("dp")
    (fh, fl), (bh, bl) = transforms(rows + taps)
    half = (rows + taps) // 2
    mixed = (out_grad[0].astype(jnp.float32) * gate_value[0].astype(jnp.float32)).astype(
        jnp.bfloat16
    )
    devices = lax.axis_size("ctx")
    rim = lax.ppermute(mixed[:taps], "ctx", [(i + 1, i) for i in range(devices - 1)])
    full_taps = lax.all_gather(filter_taps, "dp", axis=0, tiled=True)

    def spectrum(x, first=0):
        n = x.shape[0]
        s = dot(fh[:, first : first + n], x) + dot(fl[:, first : first + n], x)
        return s[:half], s[half:]

    def back(re, im, n):
        s = jnp.concatenate([re, im], 0)
        high = s.astype(jnp.bfloat16)
        low = (s - high.astype(jnp.float32)).astype(jnp.bfloat16)
        return dot(bh[:n], high) + dot(bl[:n], high) + dot(bh[:n], low)

    xr, xi = spectrum(inputs)
    gr0, gi0 = spectrum(mixed)
    gr1, gi1 = spectrum(rim, rows)
    gr, gi = gr0 + gr1, gi0 + gi1
    partial = back(xr * gr + xi * gi, xr * gi - xi * gr, taps)
    hr, hi = spectrum(full_taps)
    grad = back(hr * gr + hi * gi, hr * gi - hi * gr, rows)
    shard_grad = lax.psum(lax.psum_scatter(partial, "dp", scatter_dimension=0, tiled=True), "ctx")
    tokens_all = rows * devices * lax.axis_size("dp")
    return (grad.astype(jnp.bfloat16)[None], shard_grad * (1.0 / math.sqrt(tokens_all)))


CHUNKS = 8
EARLY = 2
FIRST = 4
MESH = pl.DeviceIdType.MESH


def kernel(
    pairs, scale,
    in_hbm, gate_hbm, cot_hbm, taps_hbm, f_hbm,
    obuf, fbuf,
    x_gc, x_in, g, inc, taps_all, f_all, xs, gs, hs, p32, own32, csrc, cbuf, half32, ysrc, ybuf,
    zsrc, zbuf, xbuf, vbuf,
    ld_gc, ld_in, ld_taps, ld_f, met, line,
    inc_s, inc_r, tz_s, tz_r, ty_s, ty_r, tc_s, tc_r,
    c_s, c_r, y_s, y_r, z_s, z_r, x_s, x_r, v_s, v_r,
):
    dp, ctx = lax.axis_index("dp"), lax.axis_index("ctx")
    core, mine = lax.rem(dp, 2), dp // 2
    partner = dp + 1 - 2 * core
    side, place, places = lax.rem(mine, 2), mine // 2, pairs // 2
    across = 2 * (mine + 1 - 2 * side) + core
    rows, channels = g.shape
    wide = channels // CHUNKS
    middle = CHUNKS // 2
    first, last = ctx == 0, ctx == 1
    other = 1 - ctx
    f32, bf = jnp.float32, jnp.bfloat16
    count = taps_all.shape[1]
    half = rows

    def cols(c):
        return pl.ds(pl.multiple_of(c * wide, wide), wide)

    def each(n, body, start=0):
        lax.fori_loop(start, n, lambda i, z: (body(i), z)[1], 0)

    def local(src, dst, sem):
        return pltpu.make_async_copy(src, dst, sem)

    def remote(src, dst, send, recv, to):
        return pltpu.make_async_remote_copy(
            src_ref=src, dst_ref=dst, send_sem=send, recv_sem=recv, device_id=to, device_id_type=MESH
        )

    own_taps = local(taps_hbm, taps_all.at[dp], ld_taps)
    load_f = local(f_hbm, f_all, ld_f)
    load_in = local(in_hbm, x_in, ld_in)

    def loads(c):
        local(cot_hbm.at[:, cols(c)], x_gc.at[0, :, cols(c)], ld_gc.at[lax.min(c, 1)]).start()
        local(gate_hbm.at[:, cols(c)], x_gc.at[1, :, cols(c)], ld_gc.at[lax.min(c, 1)]).start()

    each(CHUNKS, loads)

    barrier = pltpu.get_barrier_semaphore()

    @pl.when(first)
    def _():
        pl.semaphore_signal(barrier, inc=1, device_id=(dp, other), device_id_type=MESH)

    own_taps.start()
    load_f.start()
    load_in.start()

    @pl.when(last)
    def _():
        pl.semaphore_wait(barrier, 1)
        pl.semaphore_signal(met, inc=1, device_id=(dp, other), device_id_type=MESH)

    def z_peer(k):
        return lax.rem(place + k, places)

    def z_device(k):
        return 4 * z_peer(k) + 2 * side + core

    def rim(c):
        return remote(g.at[:, cols(c)], inc.at[:, cols(c)], inc_s, inc_r.at[c], (dp, other))

    def lend(c):
        return remote(in_hbm.at[:, cols(c)], inc.at[:, cols(c)], inc_s, inc_r.at[c], (dp, other))

    def mix(c):
        a = x_gc[0, :, cols(c)].astype(f32)
        b = x_gc[1, :, cols(c)].astype(f32)
        g[:, cols(c)] = (a * b).astype(bf)

        @pl.when(jnp.logical_and(last, jnp.logical_or(core == 0, c < FIRST)))
        def _():
            rim(c).start()

    def loaded(at, k):
        both = x_gc.at[:, :, at]
        local(both, both, ld_gc.at[k]).wait()

    loaded(pl.ds(0, wide), 0)
    mix(jnp.int32(0))
    loaded(pl.ds(wide, channels - wide), 1)
    each(CHUNKS, mix, 1)

    @pl.when(first)
    def _():
        pl.semaphore_wait(met, 1)
        pl.semaphore_signal(barrier, inc=1, device_id=(partner, ctx), device_id_type=MESH)
        pl.semaphore_signal(barrier, inc=1, device_id=(across, ctx), device_id_type=MESH)
        for k in range(1, places):
            @pl.when(z_peer(k) > place)
            def _(k=k):
                pl.semaphore_signal(barrier, inc=1, device_id=(z_device(k), ctx), device_id_type=MESH)
        each(CHUNKS, lambda c: lend(c).start(), middle)

    def ahead(which, x):
        return jnp.dot(f_all[which], jnp.concatenate([x, x], 0), preferred_element_type=f32)

    def correlate(a, b):
        ar, ai, br, bi = a[:half], a[half:], b[:half], b[half:]
        value = jnp.concatenate([ar * br + ai * bi, ar * bi - ai * br], 0)
        high = value.astype(bf)
        low = (value - high.astype(f32)).astype(bf)
        both = jnp.dot(f_all[2], high, preferred_element_type=f32)
        return both[:half] + both[half:] + jnp.dot(f_all[2, :half, :], low, preferred_element_type=f32)

    def chunk(i):
        return jnp.where(last, i, lax.rem(i + middle, CHUNKS))

    def emit(a, b, c):
        p32[...] = correlate(a, b).reshape(places, 2, 2, count, wide)
        for s in range(2):
            csrc[pl.ds(s * places, places), :, cols(c)] = p32[:, s, 1 - core].astype(bf)
            own32[pl.ds(s * places, places), :, cols(c)] = p32[:, s, core]

    def front(i):
        c = chunk(i)
        a, b = ahead(0, x_in[:, cols(c)]), ahead(0, g[:, cols(c)])
        gs[:, cols(c)] = b

        @pl.when(i < middle)
        def _():
            emit(a, b, c)

        @pl.when(i >= middle)
        def _():
            xs[:, cols(c)] = a

    def shard(p, s, c):
        return taps_all.at[4 * p + 2 * s + c]

    def tap_z(k):
        return remote(shard(place, side, core), shard(place, side, core), tz_s, tz_r.at[place], (z_device(k), ctx))

    def tap_y(p):
        return remote(shard(p, side, core), shard(p, side, core), ty_s, ty_r.at[p], (across, ctx))

    def tap_c(p, s):
        return remote(shard(p, s, core), shard(p, s, core), tc_s, tc_r, (partner, ctx))

    def tap_wait(p, s, sem):
        remote(shard(p, s, core), shard(p, s, core), tz_s, sem, (partner, ctx)).wait_recv()

    def pass_y(j):
        inner = jnp.where(j == 1, places - 1, j - 1)
        p = z_peer(jnp.where(place == 0, j, jnp.where(place == places - 1, places - j, inner)))
        tap_wait(p, side, tz_r.at[p])
        tap_y(p).start()
        tap_c(p, side).start()

    def pass_c(p):
        tap_wait(p, 1 - side, ty_r.at[p])
        tap_c(p, 1 - side).start()

    def cross(c):
        return remote(csrc.at[:, :, cols(c)], cbuf.at[:, :, cols(c)], c_s, c_r.at[c], (partner, ctx))

    def turn(c):
        return remote(ysrc.at[:, :, cols(c)], ybuf.at[:, :, cols(c)], y_s, y_r.at[c], (across, ctx))

    def spread(c, k):
        return remote(
            zsrc.at[z_peer(k), :, cols(c)], zbuf.at[place, :, cols(c)], z_s, z_r.at[c], (z_device(k), ctx)
        )

    def gathered(c):
        slots = zbuf.at[pl.ds(0, places - 1), :, cols(c)]
        return remote(slots, slots, z_s, z_r.at[c], (z_device(1), ctx))

    def swap(c):
        slot = xbuf.at[ctx, :, cols(c)]
        return remote(slot, slot, x_s, x_r, (dp, other))

    def stage2(i):
        c = chunk(i)
        cross(c).wait_recv()
        there, here = pl.ds((1 - side) * places, places), pl.ds(side * places, places)
        ysrc[:, :, cols(c)] = (own32[there, :, cols(c)] + cbuf[there, :, cols(c)].astype(f32)).astype(bf)
        turn(c).start()
        half32[:, :, cols(c)] = own32[here, :, cols(c)] + cbuf[here, :, cols(c)].astype(f32)

    def stage3(i):
        c = chunk(i)
        turn(c).wait_recv()
        total = half32[:, :, cols(c)] + ybuf[:, :, cols(c)].astype(f32)
        half32[:, :, cols(c)] = total
        zsrc[:, :, cols(c)] = total.astype(bf)
        for k in range(1, places):
            spread(c, k).start()

    def stage4(i):
        c = chunk(i)
        gathered(c).wait_recv()
        total = half32[place, :, cols(c)]
        for k in range(1, places):
            total = total + zbuf[z_peer(k), :, cols(c)].astype(f32)
        xbuf[ctx, :, cols(c)] = total.astype(bf)

        @pl.when(first)
        def _():
            swap(c).start()

    tail = chunk(CHUNKS - 1)
    theirs_tail = jnp.where(last, middle - 1, CHUNKS - 1)
    few = pl.ds(0, channels - wide)

    def direct(k, to):
        return remote(
            zsrc.at[z_peer(k), :, cols(tail)], vbuf.at[ctx * places + place], v_s, v_r, (z_device(k), to)
        )

    def finish3():
        turn(tail).wait_recv()
        total = half32[:, :, cols(tail)] + ybuf[:, :, cols(tail)].astype(f32)
        zsrc[:, :, cols(tail)] = total.astype(bf)
        for k in range(1, places):
            direct(k, other).start()
        direct(0, other).start()
        for k in range(1, places):
            direct(k, ctx).start()
        vbuf[ctx * places + place] = zsrc[place, :, cols(tail)]

    def summed(r):
        total = vbuf[r * places].astype(f32)
        for p in range(1, places):
            total = total + vbuf[r * places + p].astype(f32)
        return total.astype(bf)

    keep, drop = other.astype(f32), ctx.astype(f32)

    def arrive(c):
        remote(inc.at[:, cols(c)], inc.at[:, cols(c)], inc_s, inc_r.at[c], (dp, other)).wait_recv()
        return ahead(1, inc[:, cols(c)])

    def meet(i):
        c = chunk(i)
        w = arrive(c)
        b = gs[:, cols(c)] + keep * w
        gs[:, cols(c)] = b
        emit(xs[:, cols(c)] - drop * w, b, c)
        cross(c).start()

    def spectrum(c):
        t = taps_all[:, :, cols(c)].astype(f32).reshape(rows, wide).astype(bf)
        hs[:, cols(c)] = ahead(0, t)

    def grad(c):
        @pl.when(jnp.logical_and(first, c >= middle))
        def _():
            gs[:, cols(c)] += arrive(c)

        obuf[:, cols(c)] = correlate(hs[:, cols(c)], gs[:, cols(c)]).astype(bf)

    def at(i, when, *actions):
        @pl.when(i == when)
        def _():
            for action in actions:
                action()

    def meet_plane():
        @pl.when(first)
        def _():
            pl.semaphore_wait(barrier, 2 + place)
            pl.semaphore_signal(met, inc=1, device_id=(dp, other), device_id_type=MESH)
            for k in range(1, places):
                @pl.when(z_peer(k) < place)
                def _(k=k):
                    pl.semaphore_signal(line, inc=1, device_id=(z_device(k), ctx), device_id_type=MESH)

        @pl.when(last)
        def _():
            pl.semaphore_wait(met, 1)

        own_taps.wait()

        def lower(k):
            @pl.when(z_peer(k) < place)
            def _():
                tap_z(k).start()

        each(places, lower, 1)
        tap_y(place).start()
        tap_c(place, side).start()
        each(EARLY, lambda i: cross(chunk(i)).start())

    def meet_line():
        @pl.when(first)
        def _():
            @pl.when(place < places - 1)
            def _():
                pl.semaphore_wait(line, places - 1 - place)

            pl.semaphore_signal(line, inc=1, device_id=(dp, other), device_id_type=MESH)

        @pl.when(last)
        def _():
            pl.semaphore_wait(line, 1)

        def upper(k):
            @pl.when(z_peer(k) > place)
            def _():
                tap_z(k).start()

        each(places, upper, 1)

    def begin(i):
        front(i)

        @pl.when(jnp.logical_and(i >= EARLY, i < middle))
        def _():
            cross(chunk(i)).start()

        at(i, EARLY - 1, meet_plane)

        @pl.when(i == jnp.where(place == places - 1, EARLY - 1, jnp.where(place == 0, CHUNKS - 1, CHUNKS - 3)))
        def _():
            meet_line()

        at(i, CHUNKS - 3, lambda: each(middle, stage2))

    load_f.wait()
    load_in.wait()
    each(CHUNKS, begin)

    def follow(i):
        meet(i)
        at(i, middle, lambda: pass_y(1))
        at(i, middle + 1, lambda: each(places, pass_y, 2))
        at(i, middle + 2, lambda: each(middle, stage3))

        @pl.when(jnp.logical_and(i == CHUNKS - 1, jnp.logical_and(last, core == 1)))
        def _():
            each(CHUNKS, lambda c: rim(c).start(), FIRST)

        @pl.when(i < CHUNKS - 1)
        def _():
            stage2(i)

    each(CHUNKS, follow, middle)

    stage2(CHUNKS - 1)
    stage3(middle)
    stage3(middle + 1)
    each(places, pass_c)
    stage3(middle + 2)
    theirs = taps_all.at[pl.ds(0, pairs)]
    remote(theirs, theirs, tc_s, tc_r, (partner, ctx)).wait_recv()

    def spectra(c):
        spectrum(c)
        at(c, 3, finish3)

    each(CHUNKS, spectra)

    def swap_rest():
        @pl.when(last)
        def _():
            block = xbuf.at[ctx, :, few]
            remote(block, block, x_s, x_r, (dp, other)).start()

    def slot(c):
        grad(c)
        at(c, middle - 1, lambda: each(CHUNKS - 1, stage4), swap_rest)

    each(CHUNKS, slot)

    theirs = xbuf.at[other, :, few]
    remote(theirs, theirs, x_s, x_r, (dp, other)).wait_recv()
    theirs = vbuf.at[pl.ds(0, 2 * places - 1)]
    remote(theirs, theirs, v_s, v_r, (dp, other)).wait_recv()
    mine_x = xbuf.at[ctx, :, few]
    remote(mine_x, mine_x, x_s, x_r, (dp, other)).wait_send()
    xbuf[ctx, :, cols(tail)] = summed(ctx)
    xbuf[other, :, cols(theirs_tail)] = summed(other)
    fbuf[...] = (xbuf[0].astype(f32) + xbuf[1].astype(f32)) * scale

    def sent(ref, sem):
        remote(ref, ref, sem, x_r, (dp, other)).wait_send()

    sent(csrc, c_s)
    sent(ysrc, y_s)
    sent(zsrc.at[pl.ds(0, places - 1), :, few], z_s)
    sent(vbuf.at[pl.ds(0, 2 * places - 1)], v_s)
    sent(taps_all.at[pl.ds(0, places - 1)], tz_s)
    sent(taps_all.at[pl.ds(0, places)], ty_s)
    sent(taps_all.at[pl.ds(0, pairs)], tc_s)

    @pl.when(last)
    def _():
        sent(g, inc_s)

    @pl.when(first)
    def _():
        sent(g.at[:, pl.ds(0, channels // 2)], inc_s)


def shards(conv_input, gate_value, out_grad, filter_taps):
    _, rows, channels = conv_input.shape
    count = filter_taps.shape[0]
    members, ranks = lax.axis_size("dp"), lax.axis_size("ctx")
    taps = count * members
    wide = channels // CHUNKS
    if ranks != 2 or count % 8 or taps != rows or rows % 16 or members % 4 or channels % (128 * CHUNKS):
        return general(conv_input, gate_value, out_grad, filter_taps)
    pairs = members // 2
    places = pairs // 2
    scale = 1.0 / math.sqrt(rows * ranks * members)
    (fh, fl), (bh, bl) = transforms(rows + taps)
    matrices = np.stack([
        np.concatenate([fh[:, :rows], fl[:, :rows]], 1),
        np.concatenate([fh[:, rows:], fl[:, rows:]], 1),
        np.concatenate([bh[:rows], bl[:rows]], 0),
    ])
    hbm = pl.BlockSpec(memory_space=pltpu.HBM)
    bf, f32, dma, vmem = jnp.bfloat16, jnp.float32, pltpu.SemaphoreType.DMA, pltpu.VMEM
    out, fgrad = pl.pallas_call(
        functools.partial(kernel, pairs, scale),
        out_shape=(vmem((rows, channels), bf), vmem((count, channels), f32)),
        in_specs=[hbm] * 5,
        out_specs=(pl.BlockSpec(memory_space=vmem),) * 2,
        scratch_shapes=[
            vmem((2, rows, channels), bf),
            vmem((rows, channels), bf),
            vmem((rows, channels), bf),
            vmem((rows, channels), bf),
            vmem((members, count, channels), bf),
            vmem((3, rows + taps, rows + taps), bf),
            vmem((rows + taps, channels), f32),
            vmem((rows + taps, channels), f32),
            vmem((rows + taps, channels), f32),
            vmem((places, 2, 2, count, wide), f32),
            vmem((pairs, count, channels), f32),
            vmem((pairs, count, channels), bf),
            vmem((pairs, count, channels), bf),
            vmem((places, count, channels), f32),
            vmem((places, count, channels), bf),
            vmem((places, count, channels), bf),
            vmem((places, count, channels), bf),
            vmem((places, count, channels), bf),
            vmem((ranks, count, channels), bf),
            vmem((2 * places, count, wide), bf),
            dma((2,)), dma, dma, dma, pltpu.SemaphoreType.REGULAR, pltpu.SemaphoreType.REGULAR,
            dma, dma((CHUNKS,)), dma, dma((places,)), dma, dma((places,)), dma, dma,
            dma, dma((CHUNKS,)), dma, dma((CHUNKS,)), dma, dma((CHUNKS,)), dma, dma, dma, dma,
        ],
        compiler_params=pltpu.CompilerParams(
            collective_id=0, has_side_effects=True, vmem_limit_bytes=48_000_000
        ),
    )(*(
        pltpu.with_memory_space_constraint(x, pltpu.HBM)
        for x in (conv_input[0], gate_value[0], out_grad[0], filter_taps, jnp.asarray(matrices))
    ))
    return store(out, fgrad)


PARTS = 1


def store(grad, fgrad):
    rows, channels = grad.shape
    wide = channels // PARTS

    def body(g_ref, f_ref, g_out, f_out, sems):
        def copies():
            for k in range(PARTS):
                at = pl.ds(k * (rows // PARTS), rows // PARTS)
                yield pltpu.make_async_copy(g_ref.at[at], g_out.at[0, at], sems.at[k])
            yield pltpu.make_async_copy(f_ref, f_out, sems.at[PARTS])

        for copy in copies():
            copy.start()
        for copy in copies():
            copy.wait()

    return pl.pallas_call(
        body,
        out_shape=(
            jax.ShapeDtypeStruct((1, rows, channels), grad.dtype),
            jax.ShapeDtypeStruct(fgrad.shape, fgrad.dtype),
        ),
        in_specs=[pl.BlockSpec(memory_space=pltpu.VMEM)] * 2,
        out_specs=(pl.BlockSpec(memory_space=pl.ANY),) * 2,
        scratch_shapes=[pltpu.SemaphoreType.DMA((PARTS + 1,))],
    )(pltpu.with_memory_space_constraint(grad, pltpu.VMEM), pltpu.with_memory_space_constraint(fgrad, pltpu.VMEM))


def solution(mesh):
    in_specs = (P("dp", "ctx", None), P("dp", "ctx", None), P("dp", "ctx", None), P("dp", None))
    out_specs = (P("dp", "ctx", None), P("dp", None))
    return jax.shard_map(shards, mesh=mesh, in_specs=in_specs, out_specs=out_specs, check_vma=False)
```
